512 devices in a mesh: segment: 4 (over x), shard: 128 (over z, y, core).
Axes of the slice: x: 4, y: 4, z: 16, core: 2. Of those that a mesh axis runs over, the one named last changes fastest.
Arguments:
- item_table: bfloat16 [262144, 256], P('shard'), may hold values from -6 to 6
- user_states: bfloat16 [512, 1024], P('shard'), may hold values from -6 to 6
- w_lift: bfloat16 [4, 256, 1024], P('segment', 'shard'), may hold values from -0.375 to 0.375
- w_pair: bfloat16 [4, 1024, 2048], P('segment', 'shard'), may hold values from -0.1875 to 0.1875
- w_ask: bfloat16 [4, 1024, 1024], P('segment', 'shard'), may hold values from -0.1875 to 0.1875
- w_back: bfloat16 [4, 1024, 1024], P('segment', 'shard'), may hold values from -0.1875 to 0.1875
- norm_gains: float32 [4, 1024], P('segment'), may hold values from 0.5 to 2
- item_ids: int32 [4, 512, 128], P('segment', 'shard'), may hold values from 0 to 262143, as said below
- lengths: int32 [4, 512], P('segment', 'shard'), may hold values from 1 to 128, as said below
Outputs:
- section_states: bfloat16 [4, 512, 1024], P('segment', 'shard')
- section_scores: float32 [4, 512, 128], P('segment', 'shard')
The draws below stay inside these ranges and needn't reach their ends.
Inputs may be any that keep to these rules, and one draw needn't show every extreme that they name: `item_ids`: for every section and every micro-batch of one index of shard (2 users, 256 ids), at most 4 ids fall in any one table shard (ids j * 2048 to (j + 1) * 2048 - 1), and exactly 4 fall in one shard j that is the same for all indices of shard in that section and micro-batch. `lengths`: in every section, every micro-batch of one index of shard has a user with all 128 items live.
All inputs are finite; a program needn't handle non-finite values.
Results may differ from the reference program's by a relative error of at most 0.019.
Values may be sent and summed in bfloat16 or wider, within the bound.
No kernel may reach another device: no remote copies, remote signals or barrier semaphores. Data moves between devices by JAX's collectives and lax.ppermute only.
A program may use at most 64 MiB of HBM per device.

```python
import math
import jax
import jax.numpy as jnp
from jax import lax

D = 1024
HEADS = 8
EMB = 256
ROWS_DEV = 2048
K = 128
BU = 2
MB = 2
SECTIONS = 4
ITEMS = 262144
USERS = 512
CAP = 4


def draw_item_ids(key, part):
    shards = USERS // (MB * BU)
    block_rows = BU * K
    pool_size = shards * CAP
    hot_key, block_key = jax.random.split(jax.random.fold_in(key, 11))
    hot_owner = jax.random.randint(hot_key, (SECTIONS, 1, MB), 0, shards)
    hot_owner = jnp.broadcast_to(hot_owner, (SECTIONS, shards, MB)).reshape(-1)
    block_keys = jax.random.split(block_key, SECTIONS * shards * MB)

    def one_block(this_key, this_hot):
        first, second, third = jax.random.split(this_key, 3)
        owners = jnp.arange(pool_size, dtype=jnp.int32) // CAP
        shuffled = owners[jax.random.permutation(first, pool_size)]
        places = jnp.arange(pool_size, dtype=jnp.int32)
        ranking = jnp.where(shuffled == this_hot, places - pool_size, places)
        chosen = shuffled[jnp.argsort(ranking)][:block_rows]
        chosen = chosen[jax.random.permutation(second, block_rows)]
        offsets = jax.random.randint(third, (block_rows,), 0, ROWS_DEV)
        return chosen * ROWS_DEV + offsets
    blocks = jax.vmap(one_block)(block_keys, hot_owner)
    return blocks.reshape(SECTIONS, USERS, K).astype(jnp.int32)


def draw_lengths(key, part):
    drawn = jax.random.randint(jax.random.fold_in(key, 23), (SECTIONS, USERS // BU, BU), 1, K + 1)
    drawn = drawn.at[:, :, 0].set(K)
    return drawn.reshape(SECTIONS, USERS).astype(jnp.int32)


def steps_of(key, dims, cuts, low, top_value):
    def one(axis_at, shards_of):
        draws = jax.random.uniform(jax.random.fold_in(jax.random.fold_in(key, 6), axis_at), (shards_of,), jnp.float32, low / len(cuts), top_value / len(cuts))
        return jnp.repeat(jnp.exp(draws), dims[axis_at] // shards_of).reshape((-1,) + (1,) * (len(dims) - axis_at - 1))

    gain = one(*cuts[0])
    for cut in cuts[1:]:
        gain = gain * one(*cut)
    return gain


def centred(own_key, shape, spread, bound, pieces=(), kind=jnp.bfloat16):
    entries = jax.random.normal(own_key, shape, jnp.float32) * spread
    if len(pieces) > 0:
        entries = steps_of(own_key, shape, pieces, -0.22, 0.18) * entries
    return jnp.clip(entries, min=-bound, max=bound).astype(kind)


def setup_inputs(seed: int = 0) -> dict:
    key_list = jax.random.split(jax.random.key(seed), 10)
    item_table = centred(key_list[0], (ITEMS, EMB), 1.0, 6.0, ((0, 128),))
    user_states = centred(key_list[1], (USERS, D), 1.0, 6.0, ((0, 128),))
    w_lift = centred(key_list[2], (SECTIONS, EMB, D), EMB ** -0.5, 0.375, ((0, 4), (1, 128)))
    w_pair = centred(key_list[3], (SECTIONS, D, 2 * D), D ** -0.5, 0.1875, ((0, 4), (1, 128)))
    w_ask = centred(key_list[4], (SECTIONS, D, D), D ** -0.5, 0.1875, ((0, 4), (1, 128)))
    w_back = centred(key_list[5], (SECTIONS, D, D), D ** -0.5, 0.1875, ((0, 4), (1, 128)))
    norm_gains = jnp.clip(jnp.exp(math.log(2.0) - 1.3862944 * jax.random.uniform(key_list[6], (SECTIONS, D), jnp.float32) ** steps_of(key_list[6], (SECTIONS, D), ((0, 4),), -0.2, 0.2)), 0.5, 2.0)
    item_ids = draw_item_ids(jax.random.fold_in(key_list[9], 71), 0)
    lengths = draw_lengths(jax.random.fold_in(key_list[9], 71), 0)
    return dict(item_table=item_table, user_states=user_states, w_lift=w_lift, w_pair=w_pair, w_ask=w_ask, w_back=w_back, norm_gains=norm_gains, item_ids=item_ids, lengths=lengths)


def section(user_state, item_rows, live_mask, lift, pair, ask, back, norm_gain):
    user_count = user_state.shape[0]
    model_width = ask.shape[0]
    item_count = live_mask.shape[1]
    head_size = model_width // HEADS
    lifted = jax.nn.silu(jnp.dot(item_rows, lift, preferred_element_type=jnp.float32)).astype(jnp.bfloat16)
    paired = jnp.dot(lifted, pair, preferred_element_type=jnp.float32).astype(jnp.bfloat16)
    paired = paired.reshape(user_count, item_count, 2, HEADS, head_size).astype(jnp.float32)
    queries = jnp.dot(user_state, ask, preferred_element_type=jnp.float32).astype(jnp.bfloat16)
    queries = queries.reshape(user_count, HEADS, head_size).astype(jnp.float32)
    logits = jnp.einsum('uhd,ukhd->uhk', queries, paired[:, :, 0]) / math.sqrt(head_size)
    weights = jax.nn.silu(logits) * live_mask[:, None, :]
    item_scores = lax.optimization_barrier(jnp.mean(weights, axis=1))
    rounded = weights.astype(jnp.bfloat16).astype(jnp.float32)
    attended = jnp.einsum('uhk,ukhd->uhd', rounded, paired[:, :, 1]).reshape(user_count, model_width)
    normed = (attended * lax.rsqrt(lax.optimization_barrier(jnp.mean(attended * attended, axis=1, keepdims=True)) + 1e-05) * norm_gain).astype(jnp.bfloat16)
    update = jnp.dot(normed, back, preferred_element_type=jnp.float32)
    return ((user_state.astype(jnp.float32) + update).astype(jnp.bfloat16), item_scores)

def reference(item_table, user_states, w_lift, w_pair, w_ask, w_back, norm_gains, item_ids, lengths):
    model_width = user_states.shape[1]
    current = user_states.reshape(-1, BU, model_width)
    segment_states = []
    segment_scores = []
    for section_index in range(SECTIONS):
        wanted = item_ids[section_index].reshape(-1, BU * K)
        counts = lengths[section_index].reshape(-1, BU)

        def one_block(packed, section_index=section_index):
            block_state, block_ids, block_counts = packed
            item_rows = item_table[block_ids]
            live_mask = (jnp.arange(K, dtype=jnp.int32)[None, :] < block_counts[:, None]).astype(jnp.float32)
            return section(block_state, item_rows, live_mask, w_lift[section_index], w_pair[section_index], w_ask[section_index], w_back[section_index], norm_gains[section_index])
        current, block_scores = lax.map(one_block, (current, wanted, counts))
        segment_states.append(current.reshape(-1, model_width))
        segment_scores.append(block_scores.reshape(-1, K))
    return (jnp.stack(segment_states), jnp.stack(segment_scores))
```

```python
import math

import jax
import jax.numpy as jnp
from jax import lax
from jax.experimental import pallas as pl
from jax.experimental.pallas import tpu as pltpu
from jax.sharding import Mesh
from jax.sharding import PartitionSpec as P

HEADS = 8
BU = 2
CAP = 8
F32 = jnp.float32
BF16 = jnp.bfloat16
SHARD = ("z", "y", "core")


def vmem():
    return pl.BlockSpec(memory_space=pltpu.VMEM)


def anywhere():
    return pl.BlockSpec(memory_space=pltpu.HBM)


def request_kernel(shard_rows, ids_ref, request_ref, slot_ref):
    users, items = ids_ref.shape
    shards, capacity = request_ref.shape
    ids = ids_ref[...]
    owners = ids // shard_rows
    offsets = ids - owners * shard_rows
    owner_row = lax.broadcasted_iota(jnp.int32, (shards, items), 0)
    before = (
        lax.broadcasted_iota(jnp.int32, (items, items), 0)
        < lax.broadcasted_iota(jnp.int32, (items, items), 1)
    ).astype(BF16)
    place_row = lax.broadcasted_iota(jnp.int32, (capacity, items), 0)
    base = jnp.zeros((shards, 1), F32)
    high = jnp.zeros((shards, capacity), F32)
    low = jnp.zeros((shards, capacity), F32)
    for user in range(users):
        mine = owner_row == owners[user : user + 1, :]
        onehot = mine.astype(F32)
        onehot_low = onehot.astype(BF16)
        earlier = jnp.dot(onehot_low, before, preferred_element_type=F32) + base
        place = jnp.sum(onehot * earlier, axis=0, keepdims=True).astype(jnp.int32)
        base = base + jnp.sum(onehot, axis=1, keepdims=True)
        at_place = place_row == place
        offset = offsets[user : user + 1, :]
        offset_high = jnp.where(at_place, offset // 64, 0).astype(F32).astype(BF16)
        offset_low = jnp.where(at_place, offset % 64, 0).astype(F32).astype(BF16)
        contract = (((1,), (1,)), ((), ()))
        high = high + lax.dot_general(
            onehot_low, offset_high, contract, preferred_element_type=F32
        )
        low = low + lax.dot_general(
            onehot_low, offset_low, contract, preferred_element_type=F32
        )
        slot_ref[user : user + 1, :] = owners[user : user + 1, :] * capacity + place
    request_ref[...] = (high * 64.0 + low).astype(jnp.int32)


def table_kernel(arrived_ref, table_ref, rows_ref):
    shards, capacity, width = rows_ref.shape
    shard_rows = table_ref.shape[0]
    block = 32
    count = block * capacity
    diagonal = lax.broadcasted_iota(
        jnp.int32, (block, capacity, capacity), 1
    ) == lax.broadcasted_iota(jnp.int32, (block, capacity, capacity), 2)
    row = lax.broadcasted_iota(jnp.int32, (count, shard_rows), 1)
    for start in range(0, shards, block):
        asked = arrived_ref[start : start + block, :]
        spread = jnp.broadcast_to(asked[:, None, :], (block, capacity, capacity))
        column = jnp.sum(jnp.where(diagonal, spread, 0).astype(F32), axis=2, keepdims=True)
        column = column.astype(jnp.int32).reshape(count, 1)
        onehot = (row == column).astype(F32).astype(BF16)
        found = jnp.dot(onehot, table_ref[...], preferred_element_type=F32)
        rows_ref[start : start + block] = found.astype(BF16).reshape(block, capacity, width)


def item_kernel(
    gathered_ref,
    returned_ref,
    slot_ref,
    key_ref,
    value_ref,
    ask_ref,
    back_ref,
    pair_buf,
    lift_buf,
    ask_buf,
    back_buf,
    sems,
):
    zs, cores, ys, rows8, _ = gathered_ref.shape
    depth = zs * cores * ys * rows8
    emb = returned_ref.shape[1]
    users, items = slot_ref.shape
    width = depth
    parts = ((lift_buf, 4 * width), (pair_buf, 0), (ask_buf, 2 * width), (back_buf, 3 * width))
    copies = []
    for part, (buf, first) in enumerate(parts):
        mine = []
        for core in range(cores):
            for y in range(ys):
                copy = pltpu.make_async_copy(
                    gathered_ref.at[:, core, y, :, pl.ds(first, buf.shape[-1])],
                    buf.at[:, y, core],
                    sems.at[part, core * ys + y],
                )
                copy.start()
                mine.append(copy)
        copies.append(mine)

    slots = slot_ref[...]
    slot_row = lax.broadcasted_iota(jnp.int32, (returned_ref.shape[0], items), 0)
    returned = returned_ref[...]
    listed = []
    for user in range(users):
        onehot = (slot_row == slots[user : user + 1, :]).astype(F32).astype(BF16)
        listed.append(
            lax.dot_general(
                onehot, returned, (((0,), (0,)), ((), ())), preferred_element_type=F32
            ).astype(BF16)
        )
    listed = jnp.concatenate(listed, axis=0)

    for copy in copies[0]:
        copy.wait()
    packed = lift_buf[...].reshape(depth, emb)
    split = depth // emb
    lifted = []
    for part in range(split):
        pick = (
            lax.broadcasted_iota(jnp.int32, (emb, depth), 0) * split + part
            == lax.broadcasted_iota(jnp.int32, (emb, depth), 1)
        )
        lift = jnp.dot(
            pick.astype(F32).astype(BF16), packed, preferred_element_type=F32
        ).astype(BF16)
        lifted.append(
            jax.nn.silu(jnp.dot(listed, lift, preferred_element_type=F32)).astype(BF16)
        )
    lifted = jnp.concatenate(lifted, axis=1)
    for copy in copies[1]:
        copy.wait()
    block = 512
    for first in range(0, 2 * width, block):
        pair = pair_buf[:, :, :, :, first : first + block].reshape(depth, block)
        made = jnp.dot(lifted, pair, preferred_element_type=F32).astype(BF16)
        if first < width:
            key_ref[:, first : first + block] = made
        else:
            value_ref[:, first - width : first - width + block] = made
    for buf, ref, mine in ((ask_buf, ask_ref, copies[2]), (back_buf, back_ref, copies[3])):
        for copy in mine:
            copy.wait()
        ref[...] = buf[...].reshape(depth, width)


def section_kernel(
    state_ref, key_ref, value_ref, ask_ref, back_ref, gain_ref, length_ref, next_ref, score_ref
):
    users, width = state_ref.shape
    count = key_ref.shape[0]
    items = count // users
    head_size = width // HEADS
    rows = users * HEADS
    state = state_ref[...]
    query = jnp.dot(state, ask_ref[...], preferred_element_type=F32).astype(BF16)
    spread = jnp.broadcast_to(query.astype(F32)[:, None, :], (users, HEADS, width)).reshape(
        rows, width
    )
    in_head = (
        lax.broadcasted_iota(jnp.int32, (rows, width), 1) // head_size
        == lax.broadcasted_iota(jnp.int32, (rows, width), 0) % HEADS
    )
    spread = jnp.where(in_head, spread, 0.0).astype(BF16)
    logits = lax.dot_general(
        spread, key_ref[...], (((1,), (1,)), ((), ())), preferred_element_type=F32
    ) * (1.0 / math.sqrt(head_size))
    column = lax.broadcasted_iota(jnp.int32, (rows, count), 1)
    owner = lax.broadcasted_iota(jnp.int32, (rows, count), 0) // HEADS
    live = (column // items == owner) & (column % items < length_ref[...])
    weights = jnp.where(live, jax.nn.silu(logits), 0.0)
    score_ref[...] = jnp.sum(weights, axis=0, keepdims=True) * (1.0 / HEADS)
    mixed = jnp.dot(weights.astype(BF16), value_ref[...], preferred_element_type=F32)
    mixed = jnp.where(in_head, mixed, 0.0).reshape(users, HEADS, width)
    attended = jnp.sum(mixed, axis=1)
    scale = lax.rsqrt(jnp.mean(attended * attended, axis=1, keepdims=True) + 1e-05)
    normed = (attended * scale * gain_ref[...]).astype(BF16)
    update = jnp.dot(normed, back_ref[...], preferred_element_type=F32)
    next_ref[...] = (state.astype(F32) + update).astype(BF16)


def per_device(
    item_table, user_states, w_lift, w_pair, w_ask, w_back, norm_gains, item_ids, lengths
):
    segment_index = lax.axis_index("segment")
    segment_count = lax.axis_size("segment")
    zs, ys, cores = (lax.axis_size(name) for name in SHARD)
    shards = zs * ys * cores
    users, width = user_states.shape
    items = item_ids.shape[2]
    shard_rows, emb = item_table.shape
    depth = w_ask.shape[1]
    small, big = (pltpu.CompilerParams(vmem_limit_bytes=size << 20) for size in (12, 24))

    own = jnp.concatenate(
        [w_pair[0], w_ask[0], w_back[0], w_lift[0].reshape(depth, emb)], axis=1
    )
    near = lax.all_gather(own, "y", axis=0, tiled=True)
    gathered = lax.all_gather(near, ("z", "core"), axis=0, tiled=True)
    gathered = gathered.reshape(zs, cores, ys, depth, own.shape[1])

    request, slots = pl.pallas_call(
        lambda *refs: request_kernel(shard_rows, *refs),
        out_shape=(
            jax.ShapeDtypeStruct((shards, CAP), jnp.int32),
            jax.ShapeDtypeStruct((users, items), jnp.int32),
        ),
        in_specs=[vmem()],
        out_specs=(vmem(), vmem()),
        compiler_params=small,
        name="request",
    )(item_ids[0])
    arrived = lax.all_to_all(
        request.reshape(shards, 1, CAP), SHARD, split_axis=0, concat_axis=0, tiled=True
    )
    found = pl.pallas_call(
        table_kernel,
        out_shape=jax.ShapeDtypeStruct((shards, CAP, emb), BF16),
        in_specs=[vmem(), vmem()],
        out_specs=vmem(),
        compiler_params=small,
        name="table",
    )(arrived.reshape(shards, CAP), item_table)
    returned = lax.all_to_all(found, SHARD, split_axis=0, concat_axis=0, tiled=True)

    keys, values, ask, back = pl.pallas_call(
        item_kernel,
        out_shape=(
            jax.ShapeDtypeStruct((users * items, width), BF16),
            jax.ShapeDtypeStruct((users * items, width), BF16),
            jax.ShapeDtypeStruct((width, width), BF16),
            jax.ShapeDtypeStruct((width, width), BF16),
        ),
        in_specs=[anywhere(), vmem(), vmem()],
        out_specs=(vmem(), vmem(), vmem(), vmem()),
        scratch_shapes=[
            pltpu.VMEM((zs, ys, cores, depth, 2 * width), BF16),
            pltpu.VMEM((zs, ys, cores, depth, emb), BF16),
            pltpu.VMEM((zs, ys, cores, depth, width), BF16),
            pltpu.VMEM((zs, ys, cores, depth, width), BF16),
            pltpu.SemaphoreType.DMA((4, cores * ys)),
        ],
        compiler_params=big,
        name="item",
    )(gathered, returned.reshape(shards * CAP, emb), slots)

    length_row = jnp.repeat(lengths[0], items).reshape(1, users * items)
    section = pl.pallas_call(
        section_kernel,
        out_shape=(
            jax.ShapeDtypeStruct((users, width), BF16),
            jax.ShapeDtypeStruct((1, users * items), F32),
        ),
        in_specs=[vmem()] * 7,
        out_specs=(vmem(), vmem()),
        compiler_params=small,
        name="section",
    )
    entering = user_states
    out_state = jnp.zeros_like(user_states)
    out_score = jnp.zeros((1, users * items), F32)
    for step in range(segment_count):
        leaving, score = section(entering, keys, values, ask, back, norm_gains, length_row)
        mine = segment_index == step
        out_state = jnp.where(mine, leaving, out_state)
        out_score = jnp.where(mine, score, out_score)
        if step + 1 < segment_count:
            entering = lax.ppermute(
                leaving, "segment", [(i, i + 1) for i in range(segment_count - 1)]
            )
    return out_state[None], out_score.reshape(1, users, items)


def solution(mesh):
    split = Mesh(mesh.devices.reshape(4, 16, 4, 2), ("segment",) + SHARD)
    in_specs = (
        P(SHARD, None),
        P(SHARD, None),
        P("segment", SHARD, None),
        P("segment", SHARD, None),
        P("segment", SHARD, None),
        P("segment", SHARD, None),
        P("segment", None),
        P("segment", SHARD, None),
        P("segment", SHARD),
    )
    out_specs = (P("segment", SHARD, None), P("segment", SHARD, None))
    return jax.shard_map(
        per_device, mesh=split, in_specs=in_specs, out_specs=out_specs, check_vma=False
    )
```

```python
import math

import jax
import jax.numpy as jnp
from jax import lax
from jax.experimental import pallas as pl
from jax.experimental.pallas import tpu as pltpu
from jax.sharding import Mesh
from jax.sharding import PartitionSpec as P

HEADS = 8
BU = 2
CAP = 8
F32 = jnp.float32
BF16 = jnp.bfloat16
SHARD = ("z", "y", "core")


def vmem():
    return pl.BlockSpec(memory_space=pltpu.VMEM)


def request_kernel(shard_rows, ids_ref, request_ref, slot_ref):
    users, items = ids_ref.shape
    shards, capacity = request_ref.shape
    ids = ids_ref[...]
    owners = ids // shard_rows
    offsets = ids - owners * shard_rows
    owner_row = lax.broadcasted_iota(jnp.int32, (shards, items), 0)
    before = (
        lax.broadcasted_iota(jnp.int32, (items, items), 0)
        < lax.broadcasted_iota(jnp.int32, (items, items), 1)
    ).astype(BF16)
    place_row = lax.broadcasted_iota(jnp.int32, (capacity, items), 0)
    base = jnp.zeros((shards, 1), F32)
    high = jnp.zeros((shards, capacity), F32)
    low = jnp.zeros((shards, capacity), F32)
    for user in range(users):
        mine = owner_row == owners[user : user + 1, :]
        onehot = mine.astype(F32)
        onehot_low = onehot.astype(BF16)
        earlier = jnp.dot(onehot_low, before, preferred_element_type=F32) + base
        place = jnp.sum(onehot * earlier, axis=0, keepdims=True).astype(jnp.int32)
        base = base + jnp.sum(onehot, axis=1, keepdims=True)
        at_place = place_row == place
        offset = offsets[user : user + 1, :]
        offset_high = jnp.where(at_place, offset // 64, 0).astype(F32).astype(BF16)
        offset_low = jnp.where(at_place, offset % 64, 0).astype(F32).astype(BF16)
        contract = (((1,), (1,)), ((), ()))
        high = high + lax.dot_general(
            onehot_low, offset_high, contract, preferred_element_type=F32
        )
        low = low + lax.dot_general(
            onehot_low, offset_low, contract, preferred_element_type=F32
        )
        slot_ref[user : user + 1, :] = owners[user : user + 1, :] * capacity + place
    request_ref[...] = (high * 64.0 + low).astype(jnp.int32)


def table_kernel(arrived_ref, table_ref, rows_ref):
    shards, capacity, width = rows_ref.shape
    shard_rows = table_ref.shape[0]
    block = 32
    count = block * capacity
    diagonal = lax.broadcasted_iota(
        jnp.int32, (block, capacity, capacity), 1
    ) == lax.broadcasted_iota(jnp.int32, (block, capacity, capacity), 2)
    row = lax.broadcasted_iota(jnp.int32, (count, shard_rows), 1)
    for start in range(0, shards, block):
        asked = arrived_ref[start : start + block, :]
        spread = jnp.broadcast_to(asked[:, None, :], (block, capacity, capacity))
        column = jnp.sum(jnp.where(diagonal, spread, 0).astype(F32), axis=2, keepdims=True)
        column = column.astype(jnp.int32).reshape(count, 1)
        onehot = (row == column).astype(F32).astype(BF16)
        found = jnp.dot(onehot, table_ref[...], preferred_element_type=F32)
        rows_ref[start : start + block] = found.astype(BF16).reshape(block, capacity, width)


def list_kernel(
    count_ref,
    returned_ref,
    slot_ref,
    state_ref,
    gain_ref,
    listed_ref,
    state_out_ref,
    gain_out_ref,
    length_ref,
):
    users, items = slot_ref.shape
    state_out_ref[...] = state_ref[...]
    gain_out_ref[...] = gain_ref[...]
    owner = lax.broadcasted_iota(jnp.int32, length_ref.shape, 1) // items
    lengths = jnp.zeros(length_ref.shape, jnp.int32)
    for user in range(users):
        lengths = jnp.where(owner == user, count_ref[0, user], lengths)
    length_ref[...] = lengths
    slots = slot_ref[...]
    slot_row = lax.broadcasted_iota(jnp.int32, (returned_ref.shape[0], items), 0)
    returned = returned_ref[...]
    for user in range(users):
        onehot = (slot_row == slots[user : user + 1, :]).astype(F32).astype(BF16)
        listed_ref[user * items : (user + 1) * items, :] = lax.dot_general(
            onehot, returned, (((0,), (0,)), ((), ())), preferred_element_type=F32
        ).astype(BF16)


def section_step(state, keys, values, ask, back, gain, lengths):
    users, width = state.shape
    count = keys.shape[0]
    items = count // users
    head_size = width // HEADS
    rows = users * HEADS
    query = jnp.dot(state, ask(), preferred_element_type=F32).astype(BF16)
    spread = jnp.broadcast_to(query.astype(F32)[:, None, :], (users, HEADS, width)).reshape(
        rows, width
    )
    in_head = (
        lax.broadcasted_iota(jnp.int32, (rows, width), 1) // head_size
        == lax.broadcasted_iota(jnp.int32, (rows, width), 0) % HEADS
    )
    spread = jnp.where(in_head, spread, 0.0).astype(BF16)
    logits = lax.dot_general(
        spread, keys[...], (((1,), (1,)), ((), ())), preferred_element_type=F32
    ) * (1.0 / math.sqrt(head_size))
    column = lax.broadcasted_iota(jnp.int32, (rows, count), 1)
    owner = lax.broadcasted_iota(jnp.int32, (rows, count), 0) // HEADS
    live = (column // items == owner) & (column % items < lengths)
    weights = jnp.where(live, jax.nn.silu(logits), 0.0)
    score = jnp.sum(weights, axis=0, keepdims=True) * (1.0 / HEADS)
    mixed = jnp.dot(weights.astype(BF16), values[...], preferred_element_type=F32)
    mixed = jnp.where(in_head, mixed, 0.0).reshape(users, HEADS, width)
    attended = jnp.sum(mixed, axis=1)
    scale = lax.rsqrt(jnp.mean(attended * attended, axis=1, keepdims=True) + 1e-05)
    normed = (attended * scale * gain).astype(BF16)
    update = jnp.dot(normed, back(), preferred_element_type=F32)
    return (state.astype(F32) + update).astype(BF16), score


def item_kernel(
    gathered_ref,
    listed_ref,
    state_ref,
    gain_ref,
    length_ref,
    key_ref,
    value_ref,
    weight_ref,
    next_ref,
    score_ref,
    sems,
):
    _, cores, ys, _, columns = gathered_ref.shape
    depth, width = key_ref.shape[1], key_ref.shape[1]
    emb = listed_ref.shape[1]
    copies = []
    for part, (first, size) in enumerate(
        ((4 * width, emb), (0, 2 * width), (2 * width, 2 * width))
    ):
        mine = []
        for core in range(cores):
            for y in range(ys):
                copy = pltpu.make_async_copy(
                    gathered_ref.at[:, core, y, :, pl.ds(first, size)],
                    weight_ref.at[:, y, core, :, pl.ds(first, size)],
                    sems.at[part, core * ys + y],
                )
                copy.start()
                mine.append(copy)
        copies.append(mine)

    def weight(first, size):
        return weight_ref[:, :, :, :, first : first + size].reshape(depth, size)

    for copy in copies[0]:
        copy.wait()
    listed = listed_ref[...]
    packed = weight(4 * width, emb)
    split = depth // emb
    lifted = []
    for part in range(split):
        pick = (
            lax.broadcasted_iota(jnp.int32, (emb, depth), 0) * split + part
            == lax.broadcasted_iota(jnp.int32, (emb, depth), 1)
        )
        lift = jnp.dot(
            pick.astype(F32).astype(BF16), packed, preferred_element_type=F32
        ).astype(BF16)
        lifted.append(
            jax.nn.silu(jnp.dot(listed, lift, preferred_element_type=F32)).astype(BF16)
        )
    lifted = jnp.concatenate(lifted, axis=1)
    for copy in copies[1]:
        copy.wait()
    block = 512
    for first in range(0, 2 * width, block):
        made = jnp.dot(lifted, weight(first, block), preferred_element_type=F32).astype(BF16)
        if first < width:
            key_ref[:, first : first + block] = made
        else:
            value_ref[:, first - width : first - width + block] = made
    for copy in copies[2]:
        copy.wait()
    next_ref[...], score_ref[...] = section_step(
        state_ref[...],
        key_ref,
        value_ref,
        lambda: weight(2 * width, width),
        lambda: weight(3 * width, width),
        gain_ref[...],
        length_ref[...],
    )


def section_kernel(
    state_ref, key_ref, value_ref, weight_ref, gain_ref, length_ref, *others
):
    next_ref, score_ref = others[-2:]
    earlier = (len(others) - 2) // 2
    width = state_ref.shape[1]
    state, score = section_step(
        state_ref[...],
        key_ref,
        value_ref,
        lambda: weight_ref[:, 2 * width : 3 * width],
        lambda: weight_ref[:, 3 * width : 4 * width],
        gain_ref[...],
        length_ref[...],
    )
    segment_index = lax.axis_index("segment") if earlier else None
    for step in range(earlier):
        mine = segment_index == step
        state = jnp.where(mine, others[step][...], state)
        score = jnp.where(mine, others[earlier + step][...], score)
    next_ref[...] = state
    score_ref[...] = score


def per_device(
    item_table, user_states, w_lift, w_pair, w_ask, w_back, norm_gains, item_ids, lengths
):
    segment_count = lax.axis_size("segment")
    zs, ys, cores = (lax.axis_size(name) for name in SHARD)
    shards = zs * ys * cores
    users, width = user_states.shape
    items = item_ids.shape[2]
    shard_rows, emb = item_table.shape
    depth = w_ask.shape[1]
    small, big = (pltpu.CompilerParams(vmem_limit_bytes=size << 20) for size in (12, 38))

    own = jnp.concatenate(
        [w_pair[0], w_ask[0], w_back[0], w_lift[0].reshape(depth, emb)], axis=1
    )
    near = lax.all_gather(own, "y", axis=0, tiled=True)
    gathered = lax.all_gather(near, ("z", "core"), axis=0, tiled=True)
    gathered = gathered.reshape(zs, cores, ys, depth, own.shape[1])

    request, slots = pl.pallas_call(
        lambda *refs: request_kernel(shard_rows, *refs),
        out_shape=(
            jax.ShapeDtypeStruct((shards, CAP), jnp.int32),
            jax.ShapeDtypeStruct((users, items), jnp.int32),
        ),
        in_specs=[vmem()],
        out_specs=(vmem(), vmem()),
        compiler_params=small,
        name="request",
    )(item_ids[0])
    arrived = lax.all_to_all(
        request.reshape(shards, 1, CAP), SHARD, split_axis=0, concat_axis=0, tiled=True
    )
    found = pl.pallas_call(
        table_kernel,
        out_shape=jax.ShapeDtypeStruct((shards, CAP, emb), BF16),
        in_specs=[vmem(), vmem()],
        out_specs=vmem(),
        compiler_params=small,
        name="table",
    )(arrived.reshape(shards, CAP), item_table)
    returned = lax.all_to_all(found, SHARD, split_axis=0, concat_axis=0, tiled=True)

    smem = pl.BlockSpec(memory_space=pltpu.SMEM)
    listed, entering, gains, length_row = pl.pallas_call(
        list_kernel,
        out_shape=(
            jax.ShapeDtypeStruct((users * items, emb), BF16),
            jax.ShapeDtypeStruct(user_states.shape, BF16),
            jax.ShapeDtypeStruct(norm_gains.shape, F32),
            jax.ShapeDtypeStruct((1, users * items), jnp.int32),
        ),
        in_specs=[smem] + [vmem()] * 4,
        out_specs=(vmem(),) * 4,
        compiler_params=small,
        name="list",
    )(lengths, returned.reshape(shards * CAP, emb), slots, user_states, norm_gains)

    section_shape = (
        jax.ShapeDtypeStruct((users, width), BF16),
        jax.ShapeDtypeStruct((1, users * items), F32),
    )
    keys, values, weights, leaving, score = pl.pallas_call(
        item_kernel,
        out_shape=(
            jax.ShapeDtypeStruct((users * items, width), BF16),
            jax.ShapeDtypeStruct((users * items, width), BF16),
            jax.ShapeDtypeStruct((zs, ys, cores, depth, own.shape[1]), BF16),
        )
        + section_shape,
        in_specs=[pl.BlockSpec(memory_space=pltpu.HBM)] + [vmem()] * 4,
        out_specs=(vmem(),) * 5,
        scratch_shapes=[pltpu.SemaphoreType.DMA((3, cores * ys))],
        compiler_params=big,
        name="item",
    )(gathered, listed, entering, gains, length_row)
    weights = weights.reshape(shards * depth, own.shape[1])

    states, scores = [leaving], [score]
    for step in range(1, segment_count):
        entering = lax.ppermute(
            leaving, "segment", [(i, i + 1) for i in range(segment_count - 1)]
        )
        earlier = (*states, *scores) if step + 1 == segment_count else ()
        leaving, score = pl.pallas_call(
            section_kernel,
            out_shape=section_shape,
            in_specs=[vmem()] * (6 + len(earlier)),
            out_specs=(vmem(), vmem()),
            compiler_params=small,
            name="section",
        )(
            entering,
            keys,
            values,
            weights,
            gains,
            length_row,
            *earlier,
        )
        states.append(leaving)
        scores.append(score)
    return leaving[None], score.reshape(1, users, items)


def solution(mesh):
    split = Mesh(mesh.devices.reshape(4, 16, 4, 2), ("segment",) + SHARD)
    in_specs = (
        P(SHARD, None),
        P(SHARD, None),
        P("segment", SHARD, None),
        P("segment", SHARD, None),
        P("segment", SHARD, None),
        P("segment", SHARD, None),
        P("segment", None),
        P("segment", SHARD, None),
        P("segment", SHARD),
    )
    out_specs = (P("segment", SHARD, None), P("segment", SHARD, None))
    return jax.shard_map(
        per_device, mesh=split, in_specs=in_specs, out_specs=out_specs, check_vma=False
    )
```

```python
import math

import jax
import jax.numpy as jnp
from jax import lax
from jax.experimental import pallas as pl
from jax.experimental.pallas import tpu as pltpu
from jax.sharding import Mesh
from jax.sharding import PartitionSpec as P

HEADS = 8
BU = 2
CAP = 8
F32 = jnp.float32
BF16 = jnp.bfloat16
SHARD = ("z", "y", "core")


def vmem():
    return pl.BlockSpec(memory_space=pltpu.VMEM)


def request_kernel(shard_rows, ids_ref, request_ref, slot_ref):
    users, items = ids_ref.shape
    shards, capacity = request_ref.shape
    ids = ids_ref[...]
    owners = ids // shard_rows
    offsets = ids - owners * shard_rows
    owner_row = lax.broadcasted_iota(jnp.int32, (shards, items), 0)
    before = (
        lax.broadcasted_iota(jnp.int32, (items, items), 0)
        < lax.broadcasted_iota(jnp.int32, (items, items), 1)
    ).astype(BF16)
    place_row = lax.broadcasted_iota(jnp.int32, (capacity, items), 0)
    base = jnp.zeros((shards, 1), F32)
    high = jnp.zeros((shards, capacity), F32)
    low = jnp.zeros((shards, capacity), F32)
    for user in range(users):
        mine = owner_row == owners[user : user + 1, :]
        onehot = mine.astype(F32)
        onehot_low = onehot.astype(BF16)
        earlier = jnp.dot(onehot_low, before, preferred_element_type=F32) + base
        place = jnp.sum(onehot * earlier, axis=0, keepdims=True).astype(jnp.int32)
        base = base + jnp.sum(onehot, axis=1, keepdims=True)
        at_place = place_row == place
        offset = offsets[user : user + 1, :]
        offset_high = jnp.where(at_place, offset // 64, 0).astype(F32).astype(BF16)
        offset_low = jnp.where(at_place, offset % 64, 0).astype(F32).astype(BF16)
        contract = (((1,), (1,)), ((), ()))
        high = high + lax.dot_general(
            onehot_low, offset_high, contract, preferred_element_type=F32
        )
        low = low + lax.dot_general(
            onehot_low, offset_low, contract, preferred_element_type=F32
        )
        slot_ref[user : user + 1, :] = owners[user : user + 1, :] * capacity + place
    request_ref[...] = (high * 64.0 + low).astype(jnp.int32)


def table_kernel(arrived_ref, table_ref, rows_ref):
    shards, capacity, width = rows_ref.shape
    shard_rows = table_ref.shape[0]
    block = 32
    count = block * capacity
    diagonal = lax.broadcasted_iota(
        jnp.int32, (block, capacity, capacity), 1
    ) == lax.broadcasted_iota(jnp.int32, (block, capacity, capacity), 2)
    row = lax.broadcasted_iota(jnp.int32, (count, shard_rows), 1)
    for start in range(0, shards, block):
        asked = arrived_ref[start : start + block, :]
        spread = jnp.broadcast_to(asked[:, None, :], (block, capacity, capacity))
        column = jnp.sum(jnp.where(diagonal, spread, 0).astype(F32), axis=2, keepdims=True)
        column = column.astype(jnp.int32).reshape(count, 1)
        onehot = (row == column).astype(F32).astype(BF16)
        found = jnp.dot(onehot, table_ref[...], preferred_element_type=F32)
        rows_ref[start : start + block] = found.astype(BF16).reshape(block, capacity, width)


def list_kernel(
    count_ref,
    returned_ref,
    slot_ref,
    state_ref,
    gain_ref,
    listed_ref,
    state_out_ref,
    gain_out_ref,
    length_ref,
):
    users, items = slot_ref.shape
    state_out_ref[...] = state_ref[...]
    gain_out_ref[...] = gain_ref[...]
    owner = lax.broadcasted_iota(jnp.int32, length_ref.shape, 1) // items
    lengths = jnp.zeros(length_ref.shape, jnp.int32)
    for user in range(users):
        lengths = jnp.where(owner == user, count_ref[0, user], lengths)
    length_ref[...] = lengths
    slots = slot_ref[...]
    slot_row = lax.broadcasted_iota(jnp.int32, (returned_ref.shape[0], items), 0)
    returned = returned_ref[...]
    for user in range(users):
        onehot = (slot_row == slots[user : user + 1, :]).astype(F32).astype(BF16)
        listed_ref[user * items : (user + 1) * items, :] = lax.dot_general(
            onehot, returned, (((0,), (0,)), ((), ())), preferred_element_type=F32
        ).astype(BF16)


def section_step(state, keys, values, ask, back, gain, lengths):
    users, width = state.shape
    count = keys.shape[0]
    items = count // users
    head_size = width // HEADS
    rows = users * HEADS
    query = jnp.dot(state, ask(), preferred_element_type=F32).astype(BF16)
    spread = jnp.broadcast_to(query.astype(F32)[:, None, :], (users, HEADS, width)).reshape(
        rows, width
    )
    in_head = (
        lax.broadcasted_iota(jnp.int32, (rows, width), 1) // head_size
        == lax.broadcasted_iota(jnp.int32, (rows, width), 0) % HEADS
    )
    spread = jnp.where(in_head, spread, 0.0).astype(BF16)
    logits = lax.dot_general(
        spread, keys[...], (((1,), (1,)), ((), ())), preferred_element_type=F32
    ) * (1.0 / math.sqrt(head_size))
    column = lax.broadcasted_iota(jnp.int32, (rows, count), 1)
    owner = lax.broadcasted_iota(jnp.int32, (rows, count), 0) // HEADS
    live = (column // items == owner) & (column % items < lengths)
    weights = jnp.where(live, jax.nn.silu(logits), 0.0)
    score = jnp.sum(weights, axis=0, keepdims=True) * (1.0 / HEADS)
    mixed = jnp.dot(weights.astype(BF16), values[...], preferred_element_type=F32)
    mixed = jnp.where(in_head, mixed, 0.0).reshape(users, HEADS, width)
    attended = jnp.sum(mixed, axis=1)
    scale = lax.rsqrt(jnp.mean(attended * attended, axis=1, keepdims=True) + 1e-05)
    normed = (attended * scale * gain).astype(BF16)
    update = jnp.dot(normed, back(), preferred_element_type=F32)
    return (state.astype(F32) + update).astype(BF16), score


def item_kernel(
    gathered_ref,
    listed_ref,
    state_ref,
    gain_ref,
    length_ref,
    key_ref,
    value_ref,
    weight_ref,
    next_ref,
    score_ref,
    sems,
):
    _, cores, ys, _, columns = gathered_ref.shape
    depth, width = key_ref.shape[1], key_ref.shape[1]
    emb = listed_ref.shape[1]
    copies = []
    for part, (first, size) in enumerate(
        ((4 * width, emb), (0, 2 * width), (2 * width, 2 * width))
    ):
        mine = []
        for core in range(cores):
            for y in range(ys):
                copy = pltpu.make_async_copy(
                    gathered_ref.at[:, core, y, :, pl.ds(first, size)],
                    weight_ref.at[:, y, core, :, pl.ds(first, size)],
                    sems.at[part, core * ys + y],
                )
                copy.start()
                mine.append(copy)
        copies.append(mine)

    def weight(first, size):
        return weight_ref[:, :, :, :, first : first + size].reshape(depth, size)

    for copy in copies[0]:
        copy.wait()
    listed = listed_ref[...]
    packed = weight(4 * width, emb)
    split = depth // emb
    lifted = []
    for part in range(split):
        pick = (
            lax.broadcasted_iota(jnp.int32, (emb, depth), 0) * split + part
            == lax.broadcasted_iota(jnp.int32, (emb, depth), 1)
        )
        lift = jnp.dot(
            pick.astype(F32).astype(BF16), packed, preferred_element_type=F32
        ).astype(BF16)
        lifted.append(
            jax.nn.silu(jnp.dot(listed, lift, preferred_element_type=F32)).astype(BF16)
        )
    lifted = jnp.concatenate(lifted, axis=1)
    for copy in copies[1]:
        copy.wait()
    block = 512
    for first in range(0, 2 * width, block):
        made = jnp.dot(lifted, weight(first, block), preferred_element_type=F32).astype(BF16)
        if first < width:
            key_ref[:, first : first + block] = made
        else:
            value_ref[:, first - width : first - width + block] = made
    for copy in copies[2]:
        copy.wait()
    next_ref[...], score_ref[...] = section_step(
        state_ref[...],
        key_ref,
        value_ref,
        lambda: weight(2 * width, width),
        lambda: weight(3 * width, width),
        gain_ref[...],
        length_ref[...],
    )


def section_kernel(
    state_ref, key_ref, value_ref, weight_ref, gain_ref, length_ref, *others
):
    next_ref, score_ref = others[-2:]
    earlier = (len(others) - 2) // 2
    width = state_ref.shape[2]
    state, score = section_step(
        state_ref[0],
        key_ref,
        value_ref,
        lambda: weight_ref[:, 2 * width : 3 * width],
        lambda: weight_ref[:, 3 * width : 4 * width],
        gain_ref[...],
        length_ref[...],
    )
    segment_index = lax.axis_index("segment") if earlier else None
    for step in range(earlier):
        mine = segment_index == step
        state = jnp.where(mine, others[step][...], state)
        score = jnp.where(mine, others[earlier + step][...], score)
    next_ref[...] = state
    score_ref[...] = score


def per_device(
    item_table, user_states, w_lift, w_pair, w_ask, w_back, norm_gains, item_ids, lengths
):
    segment_count = lax.axis_size("segment")
    zs, ys, cores = (lax.axis_size(name) for name in SHARD)
    shards = zs * ys * cores
    users, width = user_states.shape
    items = item_ids.shape[2]
    shard_rows, emb = item_table.shape
    depth = w_ask.shape[1]
    small, big = (pltpu.CompilerParams(vmem_limit_bytes=size << 20) for size in (12, 38))

    own = jnp.concatenate(
        [w_pair[0], w_ask[0], w_back[0], w_lift[0].reshape(depth, emb)], axis=1
    )
    even, odd = [[0, 1], [2, 3]], [[1, 2], [0, 3]]
    near = lax.all_gather(own, "y", axis=0, tiled=True, axis_index_groups=even)
    near = lax.all_gather(near, "y", axis=0, tiled=True, axis_index_groups=odd)
    gathered = lax.all_gather(near, ("z", "core"), axis=0, tiled=True)
    gathered = gathered.reshape(zs, cores, ys, depth, own.shape[1])

    request, slots = pl.pallas_call(
        lambda *refs: request_kernel(shard_rows, *refs),
        out_shape=(
            jax.ShapeDtypeStruct((shards, CAP), jnp.int32),
            jax.ShapeDtypeStruct((users, items), jnp.int32),
        ),
        in_specs=[vmem()],
        out_specs=(vmem(), vmem()),
        compiler_params=small,
        name="request",
    )(item_ids[0])
    arrived = lax.all_to_all(
        request.reshape(shards, 1, CAP), SHARD, split_axis=0, concat_axis=0, tiled=True
    )
    found = pl.pallas_call(
        table_kernel,
        out_shape=jax.ShapeDtypeStruct((shards, CAP, emb), BF16),
        in_specs=[vmem(), vmem()],
        out_specs=vmem(),
        compiler_params=small,
        name="table",
    )(arrived.reshape(shards, CAP), item_table)
    returned = lax.all_to_all(found, SHARD, split_axis=0, concat_axis=0, tiled=True)

    smem = pl.BlockSpec(memory_space=pltpu.SMEM)
    listed, entering, gains, length_row = pl.pallas_call(
        list_kernel,
        out_shape=(
            jax.ShapeDtypeStruct((users * items, emb), BF16),
            jax.ShapeDtypeStruct(user_states.shape, BF16),
            jax.ShapeDtypeStruct(norm_gains.shape, F32),
            jax.ShapeDtypeStruct((1, users * items), jnp.int32),
        ),
        in_specs=[smem] + [vmem()] * 4,
        out_specs=(vmem(),) * 4,
        compiler_params=small,
        name="list",
    )(lengths, returned.reshape(shards * CAP, emb), slots, user_states, norm_gains)

    section_shape = (
        jax.ShapeDtypeStruct((users, width), BF16),
        jax.ShapeDtypeStruct((1, users * items), F32),
    )
    keys, values, weights, leaving, score = pl.pallas_call(
        item_kernel,
        out_shape=(
            jax.ShapeDtypeStruct((users * items, width), BF16),
            jax.ShapeDtypeStruct((users * items, width), BF16),
            jax.ShapeDtypeStruct((zs, ys, cores, depth, own.shape[1]), BF16),
        )
        + section_shape,
        in_specs=[pl.BlockSpec(memory_space=pltpu.HBM)] + [vmem()] * 4,
        out_specs=(vmem(),) * 5,
        scratch_shapes=[pltpu.SemaphoreType.DMA((3, cores * ys))],
        compiler_params=big,
        name="item",
    )(gathered, listed, entering, gains, length_row)
    weights = weights.reshape(shards * depth, own.shape[1])

    states, scores = [leaving], [score]
    for step in range(1, segment_count):
        entering = lax.all_gather(
            leaving, "segment", axis=0, axis_index_groups=even if step % 2 else odd
        )
        earlier = (*states, *scores) if step + 1 == segment_count else ()
        leaving, score = pl.pallas_call(
            section_kernel,
            out_shape=section_shape,
            in_specs=[vmem()] * (6 + len(earlier)),
            out_specs=(vmem(), vmem()),
            compiler_params=small,
            name="section",
        )(
            entering,
            keys,
            values,
            weights,
            gains,
            length_row,
            *earlier,
        )
        states.append(leaving)
        scores.append(score)
    return leaving[None], score.reshape(1, users, items)


def solution(mesh):
    split = Mesh(mesh.devices.reshape(4, 16, 4, 2), ("segment",) + SHARD)
    in_specs = (
        P(SHARD, None),
        P(SHARD, None),
        P("segment", SHARD, None),
        P("segment", SHARD, None),
        P("segment", SHARD, None),
        P("segment", SHARD, None),
        P("segment", None),
        P("segment", SHARD, None),
        P("segment", SHARD),
    )
    out_specs = (P("segment", SHARD, None), P("segment", SHARD, None))
    return jax.shard_map(
        per_device, mesh=split, in_specs=in_specs, out_specs=out_specs, check_vma=False
    )
```

```python
import math

import jax
import jax.numpy as jnp
from jax import lax
from jax.experimental import pallas as pl
from jax.experimental.pallas import tpu as pltpu
from jax.sharding import Mesh
from jax.sharding import PartitionSpec as P

HEADS = 8
BU = 2
CAP = 8
F32 = jnp.float32
BF16 = jnp.bfloat16
SHARD = ("z", "y", "core")
FROM_Z = (4, 0, -4, 8, 3, -1, -5, 7, 5, 1, -3, 9, 6, 2, -2, -6)


def vmem():
    return pl.BlockSpec(memory_space=pltpu.VMEM)


def request_kernel(shard_rows, ids_ref, request_ref, slot_ref):
    users, items = ids_ref.shape
    shards, capacity = request_ref.shape
    ids = ids_ref[...]
    owners = ids // shard_rows
    offsets = ids - owners * shard_rows
    owner_row = lax.broadcasted_iota(jnp.int32, (shards, items), 0)
    before = (
        lax.broadcasted_iota(jnp.int32, (items, items), 0)
        < lax.broadcasted_iota(jnp.int32, (items, items), 1)
    ).astype(BF16)
    place_row = lax.broadcasted_iota(jnp.int32, (capacity, items), 0)
    base = jnp.zeros((shards, 1), F32)
    high = jnp.zeros((shards, capacity), F32)
    low = jnp.zeros((shards, capacity), F32)
    for user in range(users):
        mine = owner_row == owners[user : user + 1, :]
        onehot = mine.astype(F32)
        onehot_low = onehot.astype(BF16)
        earlier = jnp.dot(onehot_low, before, preferred_element_type=F32) + base
        place = jnp.sum(onehot * earlier, axis=0, keepdims=True).astype(jnp.int32)
        base = base + jnp.sum(onehot, axis=1, keepdims=True)
        at_place = place_row == place
        offset = offsets[user : user + 1, :]
        offset_high = jnp.where(at_place, offset // 64, 0).astype(F32).astype(BF16)
        offset_low = jnp.where(at_place, offset % 64, 0).astype(F32).astype(BF16)
        contract = (((1,), (1,)), ((), ()))
        high = high + lax.dot_general(
            onehot_low, offset_high, contract, preferred_element_type=F32
        )
        low = low + lax.dot_general(
            onehot_low, offset_low, contract, preferred_element_type=F32
        )
        slot_ref[user : user + 1, :] = owners[user : user + 1, :] * capacity + place
    request_ref[...] = (high * 64.0 + low).astype(jnp.int32)


def table_kernel(arrived_ref, table_ref, rows_ref):
    shards, capacity, width = rows_ref.shape
    shard_rows = table_ref.shape[0]
    block = 32
    count = block * capacity
    diagonal = lax.broadcasted_iota(
        jnp.int32, (block, capacity, capacity), 1
    ) == lax.broadcasted_iota(jnp.int32, (block, capacity, capacity), 2)
    row = lax.broadcasted_iota(jnp.int32, (count, shard_rows), 1)
    for start in range(0, shards, block):
        asked = arrived_ref[start : start + block, :]
        spread = jnp.broadcast_to(asked[:, None, :], (block, capacity, capacity))
        column = jnp.sum(jnp.where(diagonal, spread, 0).astype(F32), axis=2, keepdims=True)
        column = column.astype(jnp.int32).reshape(count, 1)
        onehot = (row == column).astype(F32).astype(BF16)
        found = jnp.dot(onehot, table_ref[...], preferred_element_type=F32)
        rows_ref[start : start + block] = found.astype(BF16).reshape(block, capacity, width)


def list_kernel(
    count_ref,
    returned_ref,
    slot_ref,
    state_ref,
    gain_ref,
    listed_ref,
    state_out_ref,
    gain_out_ref,
    length_ref,
):
    users, items = slot_ref.shape
    state_out_ref[...] = state_ref[...]
    gain_out_ref[...] = gain_ref[...]
    owner = lax.broadcasted_iota(jnp.int32, length_ref.shape, 1) // items
    lengths = jnp.zeros(length_ref.shape, jnp.int32)
    for user in range(users):
        lengths = jnp.where(owner == user, count_ref[0, user], lengths)
    length_ref[...] = lengths
    slots = slot_ref[...]
    slot_row = lax.broadcasted_iota(jnp.int32, (returned_ref.shape[0], items), 0)
    returned = returned_ref[...]
    for user in range(users):
        onehot = (slot_row == slots[user : user + 1, :]).astype(F32).astype(BF16)
        listed_ref[user * items : (user + 1) * items, :] = lax.dot_general(
            onehot, returned, (((0,), (0,)), ((), ())), preferred_element_type=F32
        ).astype(BF16)


def section_step(state, keys, values, ask, back, gain, lengths):
    users, width = state.shape
    count = keys.shape[0]
    items = count // users
    head_size = width // HEADS
    rows = users * HEADS
    query = jnp.dot(state, ask(), preferred_element_type=F32).astype(BF16)
    spread = jnp.broadcast_to(query.astype(F32)[:, None, :], (users, HEADS, width)).reshape(
        rows, width
    )
    in_head = (
        lax.broadcasted_iota(jnp.int32, (rows, width), 1) // head_size
        == lax.broadcasted_iota(jnp.int32, (rows, width), 0) % HEADS
    )
    spread = jnp.where(in_head, spread, 0.0).astype(BF16)
    logits = lax.dot_general(
        spread, keys[...], (((1,), (1,)), ((), ())), preferred_element_type=F32
    ) * (1.0 / math.sqrt(head_size))
    column = lax.broadcasted_iota(jnp.int32, (rows, count), 1)
    owner = lax.broadcasted_iota(jnp.int32, (rows, count), 0) // HEADS
    live = (column // items == owner) & (column % items < lengths)
    weights = jnp.where(live, jax.nn.silu(logits), 0.0)
    score = jnp.sum(weights, axis=0, keepdims=True) * (1.0 / HEADS)
    mixed = jnp.dot(weights.astype(BF16), values[...], preferred_element_type=F32)
    mixed = jnp.where(in_head, mixed, 0.0).reshape(users, HEADS, width)
    attended = jnp.sum(mixed, axis=1)
    scale = lax.rsqrt(jnp.mean(attended * attended, axis=1, keepdims=True) + 1e-05)
    normed = (attended * scale * gain).astype(BF16)
    update = jnp.dot(normed, back(), preferred_element_type=F32)
    return (state.astype(F32) + update).astype(BF16), score


def item_kernel(
    *refs,
):
    pieces, refs = refs[:10], refs[10:]
    place_and_project(pieces, *refs)


def place_and_project(
    pieces,
    listed_ref,
    state_ref,
    gain_ref,
    length_ref,
    key_ref,
    value_ref,
    weight_ref,
    next_ref,
    score_ref,
    sems,
):
    zs, ys, cores, _, _ = weight_ref.shape
    depth = width = key_ref.shape[1]
    emb = listed_ref.shape[1]
    z, y, core = (lax.axis_index(name) for name in SHARD)
    half = zs // 2
    for number, piece in enumerate(pieces):
        kind, swapped = number % 5, number // 5
        first = half if kind == 4 else 0
        to_y = lax.rem(y + (0, ys - 1, 1, ys - 2, 2)[kind], ys)
        to_core = lax.rem(core + swapped, cores)
        for index in range(piece.shape[0]):
            to_z = lax.rem(z + FROM_Z[first + index] + zs, zs)
            copy = pltpu.make_async_copy(
                piece.at[index], weight_ref.at[to_z, to_y, to_core], sems.at[number]
            )
            copy.start()

    def weight(first, size):
        return weight_ref[:, :, :, :, first : first + size].reshape(depth, size)

    for number, piece in enumerate(pieces):
        whole = weight_ref.at[pl.ds(0, piece.shape[0]), 0, 0]
        pltpu.make_async_copy(piece, whole, sems.at[number]).wait()
    listed = listed_ref[...]
    packed = weight(4 * width, emb)
    split = depth // emb
    lifted = []
    for part in range(split):
        pick = (
            lax.broadcasted_iota(jnp.int32, (emb, depth), 0) * split + part
            == lax.broadcasted_iota(jnp.int32, (emb, depth), 1)
        )
        lift = jnp.dot(
            pick.astype(F32).astype(BF16), packed, preferred_element_type=F32
        ).astype(BF16)
        lifted.append(
            jax.nn.silu(jnp.dot(listed, lift, preferred_element_type=F32)).astype(BF16)
        )
    lifted = jnp.concatenate(lifted, axis=1)
    block = 512
    for first in range(0, 2 * width, block):
        made = jnp.dot(lifted, weight(first, block), preferred_element_type=F32).astype(BF16)
        if first < width:
            key_ref[:, first : first + block] = made
        else:
            value_ref[:, first - width : first - width + block] = made
    next_ref[...], score_ref[...] = section_step(
        state_ref[...],
        key_ref,
        value_ref,
        lambda: weight(2 * width, width),
        lambda: weight(3 * width, width),
        gain_ref[...],
        length_ref[...],
    )


def section_kernel(
    state_ref, key_ref, value_ref, weight_ref, gain_ref, length_ref, *others
):
    next_ref, score_ref = others[-2:]
    earlier = (len(others) - 2) // 2
    width = state_ref.shape[2]
    state, score = section_step(
        state_ref[0],
        key_ref,
        value_ref,
        lambda: weight_ref[:, 2 * width : 3 * width],
        lambda: weight_ref[:, 3 * width : 4 * width],
        gain_ref[...],
        length_ref[...],
    )
    segment_index = lax.axis_index("segment") if earlier else None
    for step in range(earlier):
        mine = segment_index == step
        state = jnp.where(mine, others[step][...], state)
        score = jnp.where(mine, others[earlier + step][...], score)
    next_ref[...] = state
    score_ref[...] = score


def per_device(
    item_table, user_states, w_lift, w_pair, w_ask, w_back, norm_gains, item_ids, lengths
):
    segment_count = lax.axis_size("segment")
    zs, ys, cores = (lax.axis_size(name) for name in SHARD)
    shards = zs * ys * cores
    users, width = user_states.shape
    items = item_ids.shape[2]
    shard_rows, emb = item_table.shape
    depth = w_ask.shape[1]
    small, big = (pltpu.CompilerParams(vmem_limit_bytes=size << 20) for size in (12, 24))

    own = jnp.concatenate(
        [w_pair[0], w_ask[0], w_back[0], w_lift[0].reshape(depth, emb)], axis=1
    )
    def moved(block, axis, distance):
        size = lax.axis_size(axis)
        return lax.ppermute(block, axis, [(i, (i + distance) % size) for i in range(size)])

    request, slots = pl.pallas_call(
        lambda *refs: request_kernel(shard_rows, *refs),
        out_shape=(
            jax.ShapeDtypeStruct((shards, CAP), jnp.int32),
            jax.ShapeDtypeStruct((users, items), jnp.int32),
        ),
        in_specs=[vmem()],
        out_specs=(vmem(), vmem()),
        compiler_params=small,
        name="request",
    )(item_ids[0])
    arrived = lax.all_to_all(
        request.reshape(shards, 1, CAP), SHARD, split_axis=0, concat_axis=0, tiled=True
    )
    own = own[None]
    far = (moved(own, "z", -4), moved(own, "z", 4), moved(own, "z", 8))
    far, arrived = lax.optimization_barrier((far, arrived))
    far = jnp.concatenate([far[0], own, *far[1:]])
    column = jnp.concatenate(
        [
            far,
            moved(far, "z", 1),
            moved(far, "z", -1),
            moved(far[:2], "z", -2),
            moved(far[1:3], "z", 2),
        ]
    )
    half = zs // 2
    below, above = moved(column, "y", 1), moved(column, "y", -1)
    across = [moved(below[:half], "y", 1), moved(above[half:], "y", -1)]
    pieces = [column, below, above, *across]
    pieces = pieces + [moved(piece, "core", 1) for piece in pieces]

    found = pl.pallas_call(
        table_kernel,
        out_shape=jax.ShapeDtypeStruct((shards, CAP, emb), BF16),
        in_specs=[vmem(), vmem()],
        out_specs=vmem(),
        compiler_params=small,
        name="table",
    )(arrived.reshape(shards, CAP), item_table)
    returned = lax.all_to_all(found, SHARD, split_axis=0, concat_axis=0, tiled=True)

    smem = pl.BlockSpec(memory_space=pltpu.SMEM)
    listed, entering, gains, length_row = pl.pallas_call(
        list_kernel,
        out_shape=(
            jax.ShapeDtypeStruct((users * items, emb), BF16),
            jax.ShapeDtypeStruct(user_states.shape, BF16),
            jax.ShapeDtypeStruct(norm_gains.shape, F32),
            jax.ShapeDtypeStruct((1, users * items), jnp.int32),
        ),
        in_specs=[smem] + [vmem()] * 4,
        out_specs=(vmem(),) * 4,
        compiler_params=small,
        name="list",
    )(lengths, returned.reshape(shards * CAP, emb), slots, user_states, norm_gains)

    section_shape = (
        jax.ShapeDtypeStruct((users, width), BF16),
        jax.ShapeDtypeStruct((1, users * items), F32),
    )
    keys, values, weights, leaving, score = pl.pallas_call(
        item_kernel,
        out_shape=(
            jax.ShapeDtypeStruct((users * items, width), BF16),
            jax.ShapeDtypeStruct((users * items, width), BF16),
            jax.ShapeDtypeStruct((zs, ys, cores, depth, own.shape[2]), BF16),
        )
        + section_shape,
        in_specs=[pl.BlockSpec(memory_space=pl.ANY)] * len(pieces) + [vmem()] * 4,
        out_specs=(vmem(),) * 5,
        scratch_shapes=[pltpu.SemaphoreType.DMA((len(pieces),))],
        compiler_params=big,
        name="item",
    )(*pieces, listed, entering, gains, length_row)
    weights = weights.reshape(shards * depth, own.shape[2])

    even, odd = [[0, 1], [2, 3]], [[1, 2], [0, 3]]
    states, scores = [leaving], [score]
    for step in range(1, segment_count):
        entering = lax.all_gather(
            leaving, "segment", axis=0, axis_index_groups=(even, odd)[step % 2 == 0]
        )
        earlier = (*states, *scores) if step + 1 == segment_count else ()
        leaving, score = pl.pallas_call(
            section_kernel,
            out_shape=section_shape,
            in_specs=[vmem()] * (6 + len(earlier)),
            out_specs=(vmem(), vmem()),
            compiler_params=small,
            name="section",
        )(
            entering,
            keys,
            values,
            weights,
            gains,
            length_row,
            *earlier,
        )
        states.append(leaving)
        scores.append(score)
    return leaving[None], score.reshape(1, users, items)


def solution(mesh):
    split = Mesh(mesh.devices.reshape(4, 16, 4, 2), ("segment",) + SHARD)
    in_specs = (
        P(SHARD, None),
        P(SHARD, None),
        P("segment", SHARD, None),
        P("segment", SHARD, None),
        P("segment", SHARD, None),
        P("segment", SHARD, None),
        P("segment", None),
        P("segment", SHARD, None),
        P("segment", SHARD),
    )
    out_specs = (P("segment", SHARD, None), P("segment", SHARD, None))
    return jax.shard_map(
        per_device, mesh=split, in_specs=in_specs, out_specs=out_specs, check_vma=False
    )
```

```python
import math

import jax
import jax.numpy as jnp
from jax import lax
from jax.experimental import pallas as pl
from jax.experimental.pallas import tpu as pltpu
from jax.sharding import Mesh
from jax.sharding import PartitionSpec as P

HEADS = 8
BU = 2
CAP = 8
F32 = jnp.float32
BF16 = jnp.bfloat16
SHARD = ("z", "y", "core")
FROM_Z = (4, 0, -4, 8, 3, -1, -5, 7, 5, 1, -3, 9, 6, 2, -2, -6)


def vmem():
    return pl.BlockSpec(memory_space=pltpu.VMEM)


def request_kernel(shard_rows, ids_ref, request_ref, slot_ref):
    users, items = ids_ref.shape
    shards, capacity = request_ref.shape
    ids = ids_ref[...]
    owners = ids // shard_rows
    offsets = ids - owners * shard_rows
    owner_row = lax.broadcasted_iota(jnp.int32, (shards, items), 0)
    before = (
        lax.broadcasted_iota(jnp.int32, (items, items), 0)
        < lax.broadcasted_iota(jnp.int32, (items, items), 1)
    ).astype(BF16)
    place_row = lax.broadcasted_iota(jnp.int32, (capacity, items), 0)
    base = jnp.zeros((shards, 1), F32)
    high = jnp.zeros((shards, capacity), F32)
    low = jnp.zeros((shards, capacity), F32)
    for user in range(users):
        mine = owner_row == owners[user : user + 1, :]
        onehot = mine.astype(F32)
        onehot_low = onehot.astype(BF16)
        earlier = jnp.dot(onehot_low, before, preferred_element_type=F32) + base
        place = jnp.sum(onehot * earlier, axis=0, keepdims=True).astype(jnp.int32)
        base = base + jnp.sum(onehot, axis=1, keepdims=True)
        at_place = place_row == place
        offset = offsets[user : user + 1, :]
        offset_high = jnp.where(at_place, offset // 64, 0).astype(F32).astype(BF16)
        offset_low = jnp.where(at_place, offset % 64, 0).astype(F32).astype(BF16)
        contract = (((1,), (1,)), ((), ()))
        high = high + lax.dot_general(
            onehot_low, offset_high, contract, preferred_element_type=F32
        )
        low = low + lax.dot_general(
            onehot_low, offset_low, contract, preferred_element_type=F32
        )
        slot_ref[user : user + 1, :] = owners[user : user + 1, :] * capacity + place
    request_ref[...] = (high * 64.0 + low).astype(jnp.int32)


def table_kernel(arrived_ref, table_ref, rows_ref):
    shards, capacity, width = rows_ref.shape
    shard_rows = table_ref.shape[0]
    block = 32
    count = block * capacity
    diagonal = lax.broadcasted_iota(
        jnp.int32, (block, capacity, capacity), 1
    ) == lax.broadcasted_iota(jnp.int32, (block, capacity, capacity), 2)
    row = lax.broadcasted_iota(jnp.int32, (count, shard_rows), 1)
    for start in range(0, shards, block):
        asked = arrived_ref[start : start + block, :]
        spread = jnp.broadcast_to(asked[:, None, :], (block, capacity, capacity))
        column = jnp.sum(jnp.where(diagonal, spread, 0).astype(F32), axis=2, keepdims=True)
        column = column.astype(jnp.int32).reshape(count, 1)
        onehot = (row == column).astype(F32).astype(BF16)
        found = jnp.dot(onehot, table_ref[...], preferred_element_type=F32)
        rows_ref[start : start + block] = found.astype(BF16).reshape(block, capacity, width)


def list_kernel(
    count_ref,
    returned_ref,
    slot_ref,
    state_ref,
    gain_ref,
    listed_ref,
    state_out_ref,
    gain_out_ref,
    length_ref,
):
    users, items = slot_ref.shape
    state_out_ref[...] = state_ref[...]
    gain_out_ref[...] = gain_ref[...]
    owner = lax.broadcasted_iota(jnp.int32, length_ref.shape, 1) // items
    lengths = jnp.zeros(length_ref.shape, jnp.int32)
    for user in range(users):
        lengths = jnp.where(owner == user, count_ref[0, user], lengths)
    length_ref[...] = lengths
    slots = slot_ref[...]
    slot_row = lax.broadcasted_iota(jnp.int32, (returned_ref.shape[0], items), 0)
    returned = returned_ref[...]
    for user in range(users):
        onehot = (slot_row == slots[user : user + 1, :]).astype(F32).astype(BF16)
        listed_ref[user * items : (user + 1) * items, :] = lax.dot_general(
            onehot, returned, (((0,), (0,)), ((), ())), preferred_element_type=F32
        ).astype(BF16)


def section_step(state, keys, values, ask, back, gain, lengths):
    users, width = state.shape
    count = keys.shape[0]
    items = count // users
    head_size = width // HEADS
    rows = users * HEADS
    query = jnp.dot(state, ask(), preferred_element_type=F32).astype(BF16)
    spread = jnp.broadcast_to(query.astype(F32)[:, None, :], (users, HEADS, width)).reshape(
        rows, width
    )
    in_head = (
        lax.broadcasted_iota(jnp.int32, (rows, width), 1) // head_size
        == lax.broadcasted_iota(jnp.int32, (rows, width), 0) % HEADS
    )
    spread = jnp.where(in_head, spread, 0.0).astype(BF16)
    logits = lax.dot_general(
        spread, keys[...], (((1,), (1,)), ((), ())), preferred_element_type=F32
    ) * (1.0 / math.sqrt(head_size))
    column = lax.broadcasted_iota(jnp.int32, (rows, count), 1)
    owner = lax.broadcasted_iota(jnp.int32, (rows, count), 0) // HEADS
    live = (column // items == owner) & (column % items < lengths)
    weights = jnp.where(live, jax.nn.silu(logits), 0.0)
    score = jnp.sum(weights, axis=0, keepdims=True) * (1.0 / HEADS)
    mixed = jnp.dot(weights.astype(BF16), values[...], preferred_element_type=F32)
    mixed = jnp.where(in_head, mixed, 0.0).reshape(users, HEADS, width)
    attended = jnp.sum(mixed, axis=1)
    scale = lax.rsqrt(jnp.mean(attended * attended, axis=1, keepdims=True) + 1e-05)
    normed = (attended * scale * gain).astype(BF16)
    update = jnp.dot(normed, back(), preferred_element_type=F32)
    return (state.astype(F32) + update).astype(BF16), score


def place(pieces, weight_ref, sems):
    zs, ys, cores, _, _ = weight_ref.shape
    z, y, core = (lax.axis_index(name) for name in SHARD)
    for number, (piece, first, from_y, swapped) in enumerate(pieces):
        to_y = lax.rem(y + from_y, ys)
        to_core = lax.rem(core + swapped, cores)
        for index in range(piece.shape[0]):
            to_z = lax.rem(z + FROM_Z[first + index] + zs, zs)
            pltpu.make_async_copy(
                piece.at[index], weight_ref.at[to_z, to_y, to_core], sems.at[number]
            ).start()


def wait_placed(pieces, weight_ref, sems):
    for number, (piece, *_) in enumerate(pieces):
        whole = weight_ref.at[pl.ds(0, piece.shape[0]), 0, 0]
        pltpu.make_async_copy(piece, whole, sems.at[number]).wait()


def place_kernel(*refs):
    *pieces, weight_ref, sems = refs
    ys = weight_ref.shape[1]
    kinds = [(piece, 0, (0, ys - 1, 1)[i % 3], i // 3) for i, piece in enumerate(pieces)]
    place(kinds, weight_ref, sems)
    wait_placed(kinds, weight_ref, sems)


def item_kernel(
    low_ref,
    high_ref,
    low_swapped_ref,
    high_swapped_ref,
    placed_ref,
    listed_ref,
    state_ref,
    gain_ref,
    length_ref,
    key_ref,
    value_ref,
    weight_ref,
    next_ref,
    score_ref,
    sems,
):
    del placed_ref
    zs = weight_ref.shape[0]
    depth = width = key_ref.shape[1]
    emb = listed_ref.shape[1]
    pieces = (low_ref, high_ref, low_swapped_ref, high_swapped_ref)
    kinds = [(piece, i % 2 * (zs // 2), 2, i // 2) for i, piece in enumerate(pieces)]
    place(kinds, weight_ref, sems)

    def weight(first, size):
        return weight_ref[:, :, :, :, first : first + size].reshape(depth, size)

    wait_placed(kinds, weight_ref, sems)
    listed = listed_ref[...]
    packed = weight(4 * width, emb)
    split = depth // emb
    lifted = []
    for part in range(split):
        pick = (
            lax.broadcasted_iota(jnp.int32, (emb, depth), 0) * split + part
            == lax.broadcasted_iota(jnp.int32, (emb, depth), 1)
        )
        lift = jnp.dot(
            pick.astype(F32).astype(BF16), packed, preferred_element_type=F32
        ).astype(BF16)
        lifted.append(
            jax.nn.silu(jnp.dot(listed, lift, preferred_element_type=F32)).astype(BF16)
        )
    lifted = jnp.concatenate(lifted, axis=1)
    block = 512
    for first in range(0, 2 * width, block):
        made = jnp.dot(lifted, weight(first, block), preferred_element_type=F32).astype(BF16)
        if first < width:
            key_ref[:, first : first + block] = made
        else:
            value_ref[:, first - width : first - width + block] = made
    next_ref[...], score_ref[...] = section_step(
        state_ref[...],
        key_ref,
        value_ref,
        lambda: weight(2 * width, width),
        lambda: weight(3 * width, width),
        gain_ref[...],
        length_ref[...],
    )


def section_kernel(
    state_ref, key_ref, value_ref, weight_ref, gain_ref, length_ref, *others
):
    next_ref, score_ref = others[-2:]
    earlier = (len(others) - 2) // 2
    width = state_ref.shape[2]
    state, score = section_step(
        state_ref[0],
        key_ref,
        value_ref,
        lambda: weight_ref[:, 2 * width : 3 * width],
        lambda: weight_ref[:, 3 * width : 4 * width],
        gain_ref[...],
        length_ref[...],
    )
    segment_index = lax.axis_index("segment") if earlier else None
    for step in range(earlier):
        mine = segment_index == step
        state = jnp.where(mine, others[step][...], state)
        score = jnp.where(mine, others[earlier + step][...], score)
    next_ref[...] = state
    score_ref[...] = score


def per_device(
    item_table, user_states, w_lift, w_pair, w_ask, w_back, norm_gains, item_ids, lengths
):
    segment_count = lax.axis_size("segment")
    zs, ys, cores = (lax.axis_size(name) for name in SHARD)
    shards = zs * ys * cores
    users, width = user_states.shape
    items = item_ids.shape[2]
    shard_rows, emb = item_table.shape
    depth = w_ask.shape[1]
    small, big = (pltpu.CompilerParams(vmem_limit_bytes=size << 20) for size in (12, 24))

    own = jnp.concatenate(
        [w_pair[0], w_ask[0], w_back[0], w_lift[0].reshape(depth, emb)], axis=1
    )
    def moved(block, axis, distance):
        size = lax.axis_size(axis)
        return lax.ppermute(block, axis, [(i, (i + distance) % size) for i in range(size)])

    request, slots = pl.pallas_call(
        lambda *refs: request_kernel(shard_rows, *refs),
        out_shape=(
            jax.ShapeDtypeStruct((shards, CAP), jnp.int32),
            jax.ShapeDtypeStruct((users, items), jnp.int32),
        ),
        in_specs=[vmem()],
        out_specs=(vmem(), vmem()),
        compiler_params=small,
        name="request",
    )(item_ids[0])
    arrived = lax.all_to_all(
        request.reshape(shards, 1, CAP), SHARD, split_axis=0, concat_axis=0, tiled=True
    )
    own = own[None]
    far = jnp.concatenate([moved(own, "z", -4), own, moved(own, "z", 4), moved(own, "z", 8)])
    near = (
        moved(far, "z", 1),
        moved(far, "z", -1),
        moved(far[:2], "z", -2),
        moved(far[1:3], "z", 2),
    )
    near, arrived = lax.optimization_barrier((near, arrived))
    column = jnp.concatenate([far, *near])
    half = zs // 2
    below, above = moved(column, "y", 1), moved(column, "y", -1)
    across = (moved(below[:half], "y", 1), moved(above[half:], "y", -1))
    both = lax.optimization_barrier((below, above))
    early = [column, below, above]
    early = early + [moved(piece, "core", 1) for piece in (column, *both)]
    found = pl.pallas_call(
        table_kernel,
        out_shape=jax.ShapeDtypeStruct((shards, CAP, emb), BF16),
        in_specs=[vmem(), vmem()],
        out_specs=vmem(),
        compiler_params=small,
        name="table",
    )(arrived.reshape(shards, CAP), item_table)
    returned = lax.all_to_all(found, SHARD, split_axis=0, concat_axis=0, tiled=True)

    early, returned = lax.optimization_barrier((early, returned))
    weights = pl.pallas_call(
        place_kernel,
        out_shape=jax.ShapeDtypeStruct((zs, ys, cores, depth, own.shape[2]), BF16),
        in_specs=[pl.BlockSpec(memory_space=pl.ANY)] * len(early),
        out_specs=vmem(),
        scratch_shapes=[pltpu.SemaphoreType.DMA((len(early),))],
        compiler_params=small,
        cost_estimate=pl.CostEstimate(flops=0, bytes_accessed=14_000_000, transcendentals=0),
        name="place",
    )(*early)
    across, weights = lax.optimization_barrier((across, weights))
    late = [*across, *(moved(piece, "core", 1) for piece in across)]

    smem = pl.BlockSpec(memory_space=pltpu.SMEM)
    listed, entering, gains, length_row = pl.pallas_call(
        list_kernel,
        out_shape=(
            jax.ShapeDtypeStruct((users * items, emb), BF16),
            jax.ShapeDtypeStruct(user_states.shape, BF16),
            jax.ShapeDtypeStruct(norm_gains.shape, F32),
            jax.ShapeDtypeStruct((1, users * items), jnp.int32),
        ),
        in_specs=[smem] + [vmem()] * 4,
        out_specs=(vmem(),) * 4,
        compiler_params=small,
        name="list",
    )(lengths, returned.reshape(shards * CAP, emb), slots, user_states, norm_gains)

    section_shape = (
        jax.ShapeDtypeStruct((users, width), BF16),
        jax.ShapeDtypeStruct((1, users * items), F32),
    )
    keys, values, weights, leaving, score = pl.pallas_call(
        item_kernel,
        out_shape=(
            jax.ShapeDtypeStruct((users * items, width), BF16),
            jax.ShapeDtypeStruct((users * items, width), BF16),
            jax.ShapeDtypeStruct((zs, ys, cores, depth, own.shape[2]), BF16),
        )
        + section_shape,
        in_specs=[pl.BlockSpec(memory_space=pl.ANY)] * 4 + [vmem()] * 5,
        out_specs=(vmem(),) * 5,
        scratch_shapes=[pltpu.SemaphoreType.DMA((len(late),))],
        input_output_aliases={4: 2},
        compiler_params=big,
        name="item",
    )(*late, weights, listed, entering, gains, length_row)
    weights = weights.reshape(shards * depth, own.shape[2])

    even, odd = [[0, 1], [2, 3]], [[1, 2], [0, 3]]
    states, scores = [leaving], [score]
    for step in range(1, segment_count):
        entering = lax.all_gather(
            leaving, "segment", axis=0, axis_index_groups=(even, odd)[step % 2 == 0]
        )
        earlier = (*states, *scores) if step + 1 == segment_count else ()
        leaving, score = pl.pallas_call(
            section_kernel,
            out_shape=section_shape,
            in_specs=[vmem()] * (6 + len(earlier)),
            out_specs=(vmem(), vmem()),
            compiler_params=small,
            name="section",
        )(
            entering,
            keys,
            values,
            weights,
            gains,
            length_row,
            *earlier,
        )
        states.append(leaving)
        scores.append(score)
    return leaving[None], score.reshape(1, users, items)


def solution(mesh):
    split = Mesh(mesh.devices.reshape(4, 16, 4, 2), ("segment",) + SHARD)
    in_specs = (
        P(SHARD, None),
        P(SHARD, None),
        P("segment", SHARD, None),
        P("segment", SHARD, None),
        P("segment", SHARD, None),
        P("segment", SHARD, None),
        P("segment", None),
        P("segment", SHARD, None),
        P("segment", SHARD),
    )
    out_specs = (P("segment", SHARD, None), P("segment", SHARD, None))
    return jax.shard_map(
        per_device, mesh=split, in_specs=in_specs, out_specs=out_specs, check_vma=False
    )
```

```python
import math

import jax
import jax.numpy as jnp
from jax import lax
from jax.experimental import pallas as pl
from jax.experimental.pallas import tpu as pltpu
from jax.sharding import Mesh
from jax.sharding import PartitionSpec as P

HEADS = 8
BU = 2
CAP = 8
F32 = jnp.float32
BF16 = jnp.bfloat16
SHARD = ("z", "y", "core")
FROM_Z = (4, 0, -4, 8, 3, -1, -5, 7, 5, 1, -3, 9, 6, 2, -2, -6)


def vmem():
    return pl.BlockSpec(memory_space=pltpu.VMEM)


def request_kernel(shard_rows, ids_ref, request_ref, slot_ref):
    users, items = ids_ref.shape
    shards, capacity = request_ref.shape
    ids = ids_ref[...]
    owners = ids // shard_rows
    offsets = ids - owners * shard_rows
    owner_row = lax.broadcasted_iota(jnp.int32, (shards, items), 0)
    before = (
        lax.broadcasted_iota(jnp.int32, (items, items), 0)
        < lax.broadcasted_iota(jnp.int32, (items, items), 1)
    ).astype(BF16)
    place_row = lax.broadcasted_iota(jnp.int32, (capacity, items), 0)
    base = jnp.zeros((shards, 1), F32)
    high = jnp.zeros((shards, capacity), F32)
    low = jnp.zeros((shards, capacity), F32)
    for user in range(users):
        mine = owner_row == owners[user : user + 1, :]
        onehot = mine.astype(F32)
        onehot_low = onehot.astype(BF16)
        earlier = jnp.dot(onehot_low, before, preferred_element_type=F32) + base
        place = jnp.sum(onehot * earlier, axis=0, keepdims=True).astype(jnp.int32)
        base = base + jnp.sum(onehot, axis=1, keepdims=True)
        at_place = place_row == place
        offset = offsets[user : user + 1, :]
        offset_high = jnp.where(at_place, offset // 64, 0).astype(F32).astype(BF16)
        offset_low = jnp.where(at_place, offset % 64, 0).astype(F32).astype(BF16)
        contract = (((1,), (1,)), ((), ()))
        high = high + lax.dot_general(
            onehot_low, offset_high, contract, preferred_element_type=F32
        )
        low = low + lax.dot_general(
            onehot_low, offset_low, contract, preferred_element_type=F32
        )
        slot_ref[user : user + 1, :] = owners[user : user + 1, :] * capacity + place
    request_ref[...] = (high * 64.0 + low).astype(jnp.int32)


def table_kernel(arrived_ref, table_ref, rows_ref):
    shards, capacity, width = rows_ref.shape
    shard_rows = table_ref.shape[0]
    block = 32
    count = block * capacity
    diagonal = lax.broadcasted_iota(
        jnp.int32, (block, capacity, capacity), 1
    ) == lax.broadcasted_iota(jnp.int32, (block, capacity, capacity), 2)
    row = lax.broadcasted_iota(jnp.int32, (count, shard_rows), 1)
    for start in range(0, shards, block):
        asked = arrived_ref[start : start + block, :]
        spread = jnp.broadcast_to(asked[:, None, :], (block, capacity, capacity))
        column = jnp.sum(jnp.where(diagonal, spread, 0).astype(F32), axis=2, keepdims=True)
        column = column.astype(jnp.int32).reshape(count, 1)
        onehot = (row == column).astype(F32).astype(BF16)
        found = jnp.dot(onehot, table_ref[...], preferred_element_type=F32)
        rows_ref[start : start + block] = found.astype(BF16).reshape(block, capacity, width)


def list_kernel(
    count_ref,
    returned_ref,
    slot_ref,
    state_ref,
    gain_ref,
    listed_ref,
    state_out_ref,
    gain_out_ref,
    length_ref,
):
    users, items = slot_ref.shape
    state_out_ref[...] = state_ref[...]
    gain_out_ref[...] = gain_ref[...]
    owner = lax.broadcasted_iota(jnp.int32, length_ref.shape, 1) // items
    lengths = jnp.zeros(length_ref.shape, jnp.int32)
    for user in range(users):
        lengths = jnp.where(owner == user, count_ref[0, user], lengths)
    length_ref[...] = lengths
    slots = slot_ref[...]
    slot_row = lax.broadcasted_iota(jnp.int32, (returned_ref.shape[0], items), 0)
    returned = returned_ref[...]
    for user in range(users):
        onehot = (slot_row == slots[user : user + 1, :]).astype(F32).astype(BF16)
        listed_ref[user * items : (user + 1) * items, :] = lax.dot_general(
            onehot, returned, (((0,), (0,)), ((), ())), preferred_element_type=F32
        ).astype(BF16)


def section_step(state, keys, values, ask, back, gain, lengths):
    users, width = state.shape
    count = keys.shape[0]
    items = count // users
    head_size = width // HEADS
    rows = users * HEADS
    query = jnp.dot(state, ask(), preferred_element_type=F32).astype(BF16)
    spread = jnp.broadcast_to(query.astype(F32)[:, None, :], (users, HEADS, width)).reshape(
        rows, width
    )
    in_head = (
        lax.broadcasted_iota(jnp.int32, (rows, width), 1) // head_size
        == lax.broadcasted_iota(jnp.int32, (rows, width), 0) % HEADS
    )
    spread = jnp.where(in_head, spread, 0.0).astype(BF16)
    logits = lax.dot_general(
        spread, keys[...], (((1,), (1,)), ((), ())), preferred_element_type=F32
    ) * (1.0 / math.sqrt(head_size))
    column = lax.broadcasted_iota(jnp.int32, (rows, count), 1)
    owner = lax.broadcasted_iota(jnp.int32, (rows, count), 0) // HEADS
    live = (column // items == owner) & (column % items < lengths)
    weights = jnp.where(live, jax.nn.silu(logits), 0.0)
    score = jnp.sum(weights, axis=0, keepdims=True) * (1.0 / HEADS)
    mixed = jnp.dot(weights.astype(BF16), values[...], preferred_element_type=F32)
    mixed = jnp.where(in_head, mixed, 0.0).reshape(users, HEADS, width)
    attended = jnp.sum(mixed, axis=1)
    scale = lax.rsqrt(jnp.mean(attended * attended, axis=1, keepdims=True) + 1e-05)
    normed = (attended * scale * gain).astype(BF16)
    update = jnp.dot(normed, back(), preferred_element_type=F32)
    return (state.astype(F32) + update).astype(BF16), score


def place(pieces, weight_ref, sems):
    zs, ys, cores, _, _ = weight_ref.shape
    z, y, core = (lax.axis_index(name) for name in SHARD)
    for number, (piece, first, from_y, swapped) in enumerate(pieces):
        to_y = lax.rem(y + from_y, ys)
        to_core = lax.rem(core + swapped, cores)
        for index in range(piece.shape[0]):
            to_z = lax.rem(z + FROM_Z[first + index] + zs, zs)
            pltpu.make_async_copy(
                piece.at[index], weight_ref.at[to_z, to_y, to_core], sems.at[number]
            ).start()


def wait_placed(pieces, weight_ref, sems):
    for number, (piece, *_) in enumerate(pieces):
        whole = weight_ref.at[pl.ds(0, piece.shape[0]), 0, 0]
        pltpu.make_async_copy(piece, whole, sems.at[number]).wait()


def place_kernel(*refs):
    *pieces, weight_ref, sems = refs
    ys = weight_ref.shape[1]
    kinds = [(piece, 0, (0, ys - 1, 1)[i % 3], i // 3) for i, piece in enumerate(pieces)]
    place(kinds, weight_ref, sems)
    wait_placed(kinds, weight_ref, sems)


def item_kernel(
    low_ref,
    high_ref,
    low_swapped_ref,
    high_swapped_ref,
    placed_ref,
    listed_ref,
    state_ref,
    gain_ref,
    length_ref,
    key_ref,
    value_ref,
    weight_ref,
    next_ref,
    score_ref,
    sems,
    load_sems,
):
    zs, ys, cores, _, _ = weight_ref.shape
    depth = width = key_ref.shape[1]
    emb = listed_ref.shape[1]
    half = zs // 2
    kinds = (
        (low_ref, 0, 2, 0),
        (high_ref, half, 2, 0),
        (low_swapped_ref, 0, 2, 1),
        (high_swapped_ref, half, 2, 1),
    )
    place(kinds, weight_ref, sems)
    y, core = lax.axis_index("y"), lax.axis_index("core")
    copies = []
    for part, (first, size) in enumerate(
        ((4 * width, emb), (0, 2 * width), (2 * width, 2 * width))
    ):
        mine = []
        for number, (from_y, from_core) in enumerate(
            (from_y, from_core) for from_y in (0, 1, ys - 1) for from_core in range(cores)
        ):
            at = (
                slice(None),
                lax.rem(y + from_y, ys),
                lax.rem(core + from_core, cores),
                slice(None),
                pl.ds(first, size),
            )
            copy = pltpu.make_async_copy(
                placed_ref.at[at], weight_ref.at[at], load_sems.at[part, number]
            )
            copy.start()
            mine.append(copy)
        copies.append(mine)

    def weight(first, size):
        return weight_ref[:, :, :, :, first : first + size].reshape(depth, size)

    wait_placed(kinds, weight_ref, sems)
    for copy in copies[0]:
        copy.wait()
    listed = listed_ref[...]
    packed = weight(4 * width, emb)
    split = depth // emb
    lifted = []
    for part in range(split):
        pick = (
            lax.broadcasted_iota(jnp.int32, (emb, depth), 0) * split + part
            == lax.broadcasted_iota(jnp.int32, (emb, depth), 1)
        )
        lift = jnp.dot(
            pick.astype(F32).astype(BF16), packed, preferred_element_type=F32
        ).astype(BF16)
        lifted.append(
            jax.nn.silu(jnp.dot(listed, lift, preferred_element_type=F32)).astype(BF16)
        )
    lifted = jnp.concatenate(lifted, axis=1)
    for copy in copies[1]:
        copy.wait()
    block = 512
    for first in range(0, 2 * width, block):
        made = jnp.dot(lifted, weight(first, block), preferred_element_type=F32).astype(BF16)
        if first < width:
            key_ref[:, first : first + block] = made
        else:
            value_ref[:, first - width : first - width + block] = made
    for copy in copies[2]:
        copy.wait()
    next_ref[...], score_ref[...] = section_step(
        state_ref[...],
        key_ref,
        value_ref,
        lambda: weight(2 * width, width),
        lambda: weight(3 * width, width),
        gain_ref[...],
        length_ref[...],
    )


def section_kernel(
    state_ref, key_ref, value_ref, weight_ref, gain_ref, length_ref, *others
):
    next_ref, score_ref = others[-2:]
    earlier = (len(others) - 2) // 2
    width = state_ref.shape[2]
    state, score = section_step(
        state_ref[0],
        key_ref,
        value_ref,
        lambda: weight_ref[:, 2 * width : 3 * width],
        lambda: weight_ref[:, 3 * width : 4 * width],
        gain_ref[...],
        length_ref[...],
    )
    segment_index = lax.axis_index("segment") if earlier else None
    for step in range(earlier):
        mine = segment_index == step
        state = jnp.where(mine, others[step][...], state)
        score = jnp.where(mine, others[earlier + step][...], score)
    next_ref[...] = state
    score_ref[...] = score


def per_device(
    item_table, user_states, w_lift, w_pair, w_ask, w_back, norm_gains, item_ids, lengths
):
    segment_count = lax.axis_size("segment")
    zs, ys, cores = (lax.axis_size(name) for name in SHARD)
    shards = zs * ys * cores
    users, width = user_states.shape
    items = item_ids.shape[2]
    shard_rows, emb = item_table.shape
    depth = w_ask.shape[1]
    small, big, wide = (pltpu.CompilerParams(vmem_limit_bytes=size << 20) for size in (12, 34, 54))

    own = jnp.concatenate(
        [w_pair[0], w_ask[0], w_back[0], w_lift[0].reshape(depth, emb)], axis=1
    )
    def moved(block, axis, distance):
        size = lax.axis_size(axis)
        return lax.ppermute(block, axis, [(i, (i + distance) % size) for i in range(size)])

    request, slots = pl.pallas_call(
        lambda *refs: request_kernel(shard_rows, *refs),
        out_shape=(
            jax.ShapeDtypeStruct((shards, CAP), jnp.int32),
            jax.ShapeDtypeStruct((users, items), jnp.int32),
        ),
        in_specs=[vmem()],
        out_specs=(vmem(), vmem()),
        compiler_params=small,
        name="request",
    )(item_ids[0])
    arrived = lax.all_to_all(
        request.reshape(shards, 1, CAP), SHARD, split_axis=0, concat_axis=0, tiled=True
    )
    own = own[None]
    far = jnp.concatenate([moved(own, "z", -4), own, moved(own, "z", 4), moved(own, "z", 8)])
    near = (
        moved(far, "z", 1),
        moved(far, "z", -1),
        moved(far[:2], "z", -2),
        moved(far[1:3], "z", 2),
    )
    near, arrived = lax.optimization_barrier((near, arrived))
    column = jnp.concatenate([far, *near])
    half = zs // 2
    below, above = moved(column, "y", 1), moved(column, "y", -1)
    across = (moved(below[:half], "y", 1), moved(above[half:], "y", -1))
    early = [column, below, above]
    early = early + [moved(piece, "core", 1) for piece in early]
    found = pl.pallas_call(
        table_kernel,
        out_shape=jax.ShapeDtypeStruct((shards, CAP, emb), BF16),
        in_specs=[vmem(), vmem()],
        out_specs=vmem(),
        compiler_params=small,
        name="table",
    )(arrived.reshape(shards, CAP), item_table)
    returned = lax.all_to_all(found, SHARD, split_axis=0, concat_axis=0, tiled=True)

    weights = pl.pallas_call(
        place_kernel,
        out_shape=jax.ShapeDtypeStruct((zs, ys, cores, depth, own.shape[2]), BF16),
        in_specs=[pl.BlockSpec(memory_space=pl.ANY)] * len(early),
        out_specs=pl.BlockSpec(memory_space=pltpu.HBM),
        scratch_shapes=[pltpu.SemaphoreType.DMA((len(early),))],
        compiler_params=wide,
        cost_estimate=pl.CostEstimate(flops=0, bytes_accessed=14_000_000, transcendentals=0),
        name="place",
    )(*early)
    across, weights = lax.optimization_barrier((across, weights))
    late = [*across, *(moved(piece, "core", 1) for piece in across)]

    smem = pl.BlockSpec(memory_space=pltpu.SMEM)
    listed, entering, gains, length_row = pl.pallas_call(
        list_kernel,
        out_shape=(
            jax.ShapeDtypeStruct((users * items, emb), BF16),
            jax.ShapeDtypeStruct(user_states.shape, BF16),
            jax.ShapeDtypeStruct(norm_gains.shape, F32),
            jax.ShapeDtypeStruct((1, users * items), jnp.int32),
        ),
        in_specs=[smem] + [vmem()] * 4,
        out_specs=(vmem(),) * 4,
        compiler_params=small,
        name="list",
    )(lengths, returned.reshape(shards * CAP, emb), slots, user_states, norm_gains)

    section_shape = (
        jax.ShapeDtypeStruct((users, width), BF16),
        jax.ShapeDtypeStruct((1, users * items), F32),
    )
    keys, values, weights, leaving, score = pl.pallas_call(
        item_kernel,
        out_shape=(
            jax.ShapeDtypeStruct((users * items, width), BF16),
            jax.ShapeDtypeStruct((users * items, width), BF16),
            jax.ShapeDtypeStruct((zs, ys, cores, depth, own.shape[2]), BF16),
        )
        + section_shape,
        in_specs=[pl.BlockSpec(memory_space=pl.ANY)] * len(late)
        + [pl.BlockSpec(memory_space=pltpu.HBM)]
        + [vmem()] * 4,
        out_specs=(vmem(),) * 5,
        scratch_shapes=[
            pltpu.SemaphoreType.DMA((len(late),)),
            pltpu.SemaphoreType.DMA((3, 6)),
        ],
        compiler_params=big,
        name="item",
    )(*late, weights, listed, entering, gains, length_row)
    weights = weights.reshape(shards * depth, own.shape[2])

    even, odd = [[0, 1], [2, 3]], [[1, 2], [0, 3]]
    states, scores = [leaving], [score]
    for step in range(1, segment_count):
        entering = lax.all_gather(
            leaving, "segment", axis=0, axis_index_groups=(even, odd)[step % 2 == 0]
        )
        earlier = (*states, *scores) if step + 1 == segment_count else ()
        leaving, score = pl.pallas_call(
            section_kernel,
            out_shape=section_shape,
            in_specs=[vmem()] * (6 + len(earlier)),
            out_specs=(vmem(), vmem()),
            compiler_params=small,
            name="section",
        )(
            entering,
            keys,
            values,
            weights,
            gains,
            length_row,
            *earlier,
        )
        states.append(leaving)
        scores.append(score)
    return leaving[None], score.reshape(1, users, items)


def solution(mesh):
    split = Mesh(mesh.devices.reshape(4, 16, 4, 2), ("segment",) + SHARD)
    in_specs = (
        P(SHARD, None),
        P(SHARD, None),
        P("segment", SHARD, None),
        P("segment", SHARD, None),
        P("segment", SHARD, None),
        P("segment", SHARD, None),
        P("segment", None),
        P("segment", SHARD, None),
        P("segment", SHARD),
    )
    out_specs = (P("segment", SHARD, None), P("segment", SHARD, None))
    return jax.shard_map(
        per_device, mesh=split, in_specs=in_specs, out_specs=out_specs, check_vma=False
    )
```

```python
import math

import jax
import jax.numpy as jnp
from jax import lax
from jax.experimental import pallas as pl
from jax.experimental.pallas import tpu as pltpu
from jax.sharding import Mesh
from jax.sharding import PartitionSpec as P

HEADS = 8
BU = 2
CAP = 8
F32 = jnp.float32
BF16 = jnp.bfloat16
SHARD = ("z", "y", "core")
FROM_Z = (4, 0, -4, 8, 3, -1, -5, 7, 5, 1, -3, 9, 6, 2, -2, -6)


def vmem():
    return pl.BlockSpec(memory_space=pltpu.VMEM)


def request_kernel(shard_rows, ids_ref, request_ref, slot_ref):
    users, items = ids_ref.shape
    shards, capacity = request_ref.shape
    ids = ids_ref[...]
    owners = ids // shard_rows
    offsets = ids - owners * shard_rows
    owner_row = lax.broadcasted_iota(jnp.int32, (shards, items), 0)
    before = (
        lax.broadcasted_iota(jnp.int32, (items, items), 0)
        < lax.broadcasted_iota(jnp.int32, (items, items), 1)
    ).astype(BF16)
    place_row = lax.broadcasted_iota(jnp.int32, (capacity, items), 0)
    base = jnp.zeros((shards, 1), F32)
    high = jnp.zeros((shards, capacity), F32)
    low = jnp.zeros((shards, capacity), F32)
    for user in range(users):
        mine = owner_row == owners[user : user + 1, :]
        onehot = mine.astype(F32)
        onehot_low = onehot.astype(BF16)
        earlier = jnp.dot(onehot_low, before, preferred_element_type=F32) + base
        place = jnp.sum(onehot * earlier, axis=0, keepdims=True).astype(jnp.int32)
        base = base + jnp.sum(onehot, axis=1, keepdims=True)
        at_place = place_row == place
        offset = offsets[user : user + 1, :]
        offset_high = jnp.where(at_place, offset // 64, 0).astype(F32).astype(BF16)
        offset_low = jnp.where(at_place, offset % 64, 0).astype(F32).astype(BF16)
        contract = (((1,), (1,)), ((), ()))
        high = high + lax.dot_general(
            onehot_low, offset_high, contract, preferred_element_type=F32
        )
        low = low + lax.dot_general(
            onehot_low, offset_low, contract, preferred_element_type=F32
        )
        slot_ref[user : user + 1, :] = owners[user : user + 1, :] * capacity + place
    request_ref[...] = (high * 64.0 + low).astype(jnp.int32)


def table_kernel(arrived_ref, table_ref, rows_ref):
    shards, capacity, width = rows_ref.shape
    shard_rows = table_ref.shape[0]
    block = 32
    count = block * capacity
    diagonal = lax.broadcasted_iota(
        jnp.int32, (block, capacity, capacity), 1
    ) == lax.broadcasted_iota(jnp.int32, (block, capacity, capacity), 2)
    row = lax.broadcasted_iota(jnp.int32, (count, shard_rows), 1)
    for start in range(0, shards, block):
        asked = arrived_ref[start : start + block, :]
        spread = jnp.broadcast_to(asked[:, None, :], (block, capacity, capacity))
        column = jnp.sum(jnp.where(diagonal, spread, 0).astype(F32), axis=2, keepdims=True)
        column = column.astype(jnp.int32).reshape(count, 1)
        onehot = (row == column).astype(F32).astype(BF16)
        found = jnp.dot(onehot, table_ref[...], preferred_element_type=F32)
        rows_ref[start : start + block] = found.astype(BF16).reshape(block, capacity, width)


def list_kernel(
    count_ref,
    returned_ref,
    slot_ref,
    state_ref,
    gain_ref,
    listed_ref,
    state_out_ref,
    gain_out_ref,
    length_ref,
):
    users, items = slot_ref.shape
    state_out_ref[...] = state_ref[...]
    gain_out_ref[...] = gain_ref[...]
    owner = lax.broadcasted_iota(jnp.int32, length_ref.shape, 1) // items
    lengths = jnp.zeros(length_ref.shape, jnp.int32)
    for user in range(users):
        lengths = jnp.where(owner == user, count_ref[0, user], lengths)
    length_ref[...] = lengths
    slots = slot_ref[...]
    slot_row = lax.broadcasted_iota(jnp.int32, (returned_ref.shape[0], items), 0)
    returned = returned_ref[...]
    for user in range(users):
        onehot = (slot_row == slots[user : user + 1, :]).astype(F32).astype(BF16)
        listed_ref[user * items : (user + 1) * items, :] = lax.dot_general(
            onehot, returned, (((0,), (0,)), ((), ())), preferred_element_type=F32
        ).astype(BF16)


def section_step(state, keys, values, ask, back, gain, lengths):
    users, width = state.shape
    count = keys.shape[0]
    items = count // users
    head_size = width // HEADS
    rows = users * HEADS
    query = jnp.dot(state, ask(), preferred_element_type=F32).astype(BF16)
    spread = jnp.broadcast_to(query.astype(F32)[:, None, :], (users, HEADS, width)).reshape(
        rows, width
    )
    in_head = (
        lax.broadcasted_iota(jnp.int32, (rows, width), 1) // head_size
        == lax.broadcasted_iota(jnp.int32, (rows, width), 0) % HEADS
    )
    spread = jnp.where(in_head, spread, 0.0).astype(BF16)
    logits = lax.dot_general(
        spread, keys[...], (((1,), (1,)), ((), ())), preferred_element_type=F32
    ) * (1.0 / math.sqrt(head_size))
    column = lax.broadcasted_iota(jnp.int32, (rows, count), 1)
    owner = lax.broadcasted_iota(jnp.int32, (rows, count), 0) // HEADS
    live = (column // items == owner) & (column % items < lengths)
    weights = jnp.where(live, jax.nn.silu(logits), 0.0)
    score = jnp.sum(weights, axis=0, keepdims=True) * (1.0 / HEADS)
    mixed = jnp.dot(weights.astype(BF16), values[...], preferred_element_type=F32)
    mixed = jnp.where(in_head, mixed, 0.0).reshape(users, HEADS, width)
    attended = jnp.sum(mixed, axis=1)
    scale = lax.rsqrt(jnp.mean(attended * attended, axis=1, keepdims=True) + 1e-05)
    normed = (attended * scale * gain).astype(BF16)
    update = jnp.dot(normed, back(), preferred_element_type=F32)
    return (state.astype(F32) + update).astype(BF16), score


def place(pieces, weight_ref, sems):
    zs, ys, cores, _, _ = weight_ref.shape
    z, y, core = (lax.axis_index(name) for name in SHARD)
    for number, (piece, first, from_y, swapped) in enumerate(pieces):
        to_y = lax.rem(y + from_y, ys)
        to_core = lax.rem(core + swapped, cores)
        for index in range(piece.shape[0]):
            to_z = lax.rem(z + FROM_Z[first + index] + zs, zs)
            pltpu.make_async_copy(
                piece.at[index], weight_ref.at[to_z, to_y, to_core], sems.at[number]
            ).start()


def wait_placed(pieces, weight_ref, sems):
    for number, (piece, *_) in enumerate(pieces):
        whole = weight_ref.at[pl.ds(0, piece.shape[0]), 0, 0]
        pltpu.make_async_copy(piece, whole, sems.at[number]).wait()


def place_kernel(*refs):
    *pieces, weight_ref, sems = refs
    ys = weight_ref.shape[1]
    parts = ((ys - 1, 0), (1, 0), (ys - 1, 1), (1, 1), (0, 1))
    kinds = [(piece, 0, *part) for piece, part in zip(pieces, parts)]
    place(kinds, weight_ref, sems)
    wait_placed(kinds, weight_ref, sems)


def item_kernel(
    column_ref,
    low_ref,
    high_ref,
    low_swapped_ref,
    high_swapped_ref,
    placed_ref,
    listed_ref,
    state_ref,
    gain_ref,
    length_ref,
    key_ref,
    value_ref,
    weight_ref,
    next_ref,
    score_ref,
    sems,
    load_sems,
):
    zs, ys, cores, _, _ = weight_ref.shape
    depth = width = key_ref.shape[1]
    emb = listed_ref.shape[1]
    half = zs // 2
    kinds = (
        (column_ref, 0, 0, 0),
        (low_ref, 0, 2, 0),
        (high_ref, half, 2, 0),
        (low_swapped_ref, 0, 2, 1),
        (high_swapped_ref, half, 2, 1),
    )
    place(kinds, weight_ref, sems)
    y, core = lax.axis_index("y"), lax.axis_index("core")
    copies = []
    for part, (first, size) in enumerate(
        ((4 * width, emb), (0, 2 * width), (2 * width, 2 * width))
    ):
        mine = []
        for number, (from_y, from_core) in enumerate(
            ((ys - 1, 0), (1, 0), (ys - 1, 1), (1, 1), (0, 1))
        ):
            at = (
                slice(None),
                lax.rem(y + from_y, ys),
                lax.rem(core + from_core, cores),
                slice(None),
                pl.ds(first, size),
            )
            copy = pltpu.make_async_copy(
                placed_ref.at[at], weight_ref.at[at], load_sems.at[part, number]
            )
            copy.start()
            mine.append(copy)
        copies.append(mine)

    def weight(first, size):
        return weight_ref[:, :, :, :, first : first + size].reshape(depth, size)

    wait_placed(kinds, weight_ref, sems)
    for copy in copies[0]:
        copy.wait()
    listed = listed_ref[...]
    packed = weight(4 * width, emb)
    split = depth // emb
    lifted = []
    for part in range(split):
        pick = (
            lax.broadcasted_iota(jnp.int32, (emb, depth), 0) * split + part
            == lax.broadcasted_iota(jnp.int32, (emb, depth), 1)
        )
        lift = jnp.dot(
            pick.astype(F32).astype(BF16), packed, preferred_element_type=F32
        ).astype(BF16)
        lifted.append(
            jax.nn.silu(jnp.dot(listed, lift, preferred_element_type=F32)).astype(BF16)
        )
    lifted = jnp.concatenate(lifted, axis=1)
    for copy in copies[1]:
        copy.wait()
    block = 512
    for first in range(0, 2 * width, block):
        made = jnp.dot(lifted, weight(first, block), preferred_element_type=F32).astype(BF16)
        if first < width:
            key_ref[:, first : first + block] = made
        else:
            value_ref[:, first - width : first - width + block] = made
    for copy in copies[2]:
        copy.wait()
    next_ref[...], score_ref[...] = section_step(
        state_ref[...],
        key_ref,
        value_ref,
        lambda: weight(2 * width, width),
        lambda: weight(3 * width, width),
        gain_ref[...],
        length_ref[...],
    )


def section_kernel(
    state_ref, key_ref, value_ref, weight_ref, gain_ref, length_ref, *others
):
    next_ref, score_ref = others[-2:]
    earlier = (len(others) - 2) // 2
    width = state_ref.shape[2]
    state, score = section_step(
        state_ref[0],
        key_ref,
        value_ref,
        lambda: weight_ref[:, 2 * width : 3 * width],
        lambda: weight_ref[:, 3 * width : 4 * width],
        gain_ref[...],
        length_ref[...],
    )
    segment_index = lax.axis_index("segment") if earlier else None
    for step in range(earlier):
        mine = segment_index == step
        state = jnp.where(mine, others[step][...], state)
        score = jnp.where(mine, others[earlier + step][...], score)
    next_ref[...] = state
    score_ref[...] = score


def per_device(
    item_table, user_states, w_lift, w_pair, w_ask, w_back, norm_gains, item_ids, lengths
):
    segment_count = lax.axis_size("segment")
    zs, ys, cores = (lax.axis_size(name) for name in SHARD)
    shards = zs * ys * cores
    users, width = user_states.shape
    items = item_ids.shape[2]
    shard_rows, emb = item_table.shape
    depth = w_ask.shape[1]
    small, big, wide = (pltpu.CompilerParams(vmem_limit_bytes=size << 20) for size in (12, 34, 44))

    own = jnp.concatenate(
        [w_pair[0], w_ask[0], w_back[0], w_lift[0].reshape(depth, emb)], axis=1
    )
    def moved(block, axis, distance):
        size = lax.axis_size(axis)
        return lax.ppermute(block, axis, [(i, (i + distance) % size) for i in range(size)])

    request, slots = pl.pallas_call(
        lambda *refs: request_kernel(shard_rows, *refs),
        out_shape=(
            jax.ShapeDtypeStruct((shards, CAP), jnp.int32),
            jax.ShapeDtypeStruct((users, items), jnp.int32),
        ),
        in_specs=[vmem()],
        out_specs=(vmem(), vmem()),
        compiler_params=small,
        name="request",
    )(item_ids[0])
    arrived = lax.all_to_all(
        request.reshape(shards, 1, CAP), SHARD, split_axis=0, concat_axis=0, tiled=True
    )
    own = own[None]
    far = jnp.concatenate([moved(own, "z", -4), own, moved(own, "z", 4), moved(own, "z", 8)])
    near = (
        moved(far, "z", 1),
        moved(far, "z", -1),
        moved(far[:2], "z", -2),
        moved(far[1:3], "z", 2),
    )
    near, arrived = lax.optimization_barrier((near, arrived))
    column = jnp.concatenate([far, *near])
    half = zs // 2
    below, above = moved(column, "y", 1), moved(column, "y", -1)
    across = (moved(below[:half], "y", 1), moved(above[half:], "y", -1))
    early = [below, above]
    early = early + [moved(piece, "core", 1) for piece in (below, above, column)]
    found = pl.pallas_call(
        table_kernel,
        out_shape=jax.ShapeDtypeStruct((shards, CAP, emb), BF16),
        in_specs=[vmem(), vmem()],
        out_specs=vmem(),
        compiler_params=small,
        name="table",
    )(arrived.reshape(shards, CAP), item_table)
    returned = lax.all_to_all(found, SHARD, split_axis=0, concat_axis=0, tiled=True)

    weights = pl.pallas_call(
        place_kernel,
        out_shape=jax.ShapeDtypeStruct((zs, ys, cores, depth, own.shape[2]), BF16),
        in_specs=[pl.BlockSpec(memory_space=pl.ANY)] * len(early),
        out_specs=pl.BlockSpec(memory_space=pltpu.HBM),
        scratch_shapes=[pltpu.SemaphoreType.DMA((len(early),))],
        compiler_params=wide,
        cost_estimate=pl.CostEstimate(flops=0, bytes_accessed=14_000_000, transcendentals=0),
        name="place",
    )(*early)
    across, weights = lax.optimization_barrier((across, weights))
    late = [column, *across, *(moved(piece, "core", 1) for piece in across)]

    smem = pl.BlockSpec(memory_space=pltpu.SMEM)
    listed, entering, gains, length_row = pl.pallas_call(
        list_kernel,
        out_shape=(
            jax.ShapeDtypeStruct((users * items, emb), BF16),
            jax.ShapeDtypeStruct(user_states.shape, BF16),
            jax.ShapeDtypeStruct(norm_gains.shape, F32),
            jax.ShapeDtypeStruct((1, users * items), jnp.int32),
        ),
        in_specs=[smem] + [vmem()] * 4,
        out_specs=(vmem(),) * 4,
        compiler_params=small,
        name="list",
    )(lengths, returned.reshape(shards * CAP, emb), slots, user_states, norm_gains)

    section_shape = (
        jax.ShapeDtypeStruct((users, width), BF16),
        jax.ShapeDtypeStruct((1, users * items), F32),
    )
    keys, values, weights, leaving, score = pl.pallas_call(
        item_kernel,
        out_shape=(
            jax.ShapeDtypeStruct((users * items, width), BF16),
            jax.ShapeDtypeStruct((users * items, width), BF16),
            jax.ShapeDtypeStruct((zs, ys, cores, depth, own.shape[2]), BF16),
        )
        + section_shape,
        in_specs=[pl.BlockSpec(memory_space=pl.ANY)] * len(late)
        + [pl.BlockSpec(memory_space=pltpu.HBM)]
        + [vmem()] * 4,
        out_specs=(vmem(),) * 5,
        scratch_shapes=[
            pltpu.SemaphoreType.DMA((len(late),)),
            pltpu.SemaphoreType.DMA((3, 5)),
        ],
        compiler_params=big,
        name="item",
    )(*late, weights, listed, entering, gains, length_row)
    weights = weights.reshape(shards * depth, own.shape[2])

    even, odd = [[0, 1], [2, 3]], [[1, 2], [0, 3]]
    states, scores = [leaving], [score]
    for step in range(1, segment_count):
        entering = lax.all_gather(
            leaving, "segment", axis=0, axis_index_groups=(even, odd)[step % 2 == 0]
        )
        earlier = (*states, *scores) if step + 1 == segment_count else ()
        leaving, score = pl.pallas_call(
            section_kernel,
            out_shape=section_shape,
            in_specs=[vmem()] * (6 + len(earlier)),
            out_specs=(vmem(), vmem()),
            compiler_params=small,
            name="section",
        )(
            entering,
            keys,
            values,
            weights,
            gains,
            length_row,
            *earlier,
        )
        states.append(leaving)
        scores.append(score)
    return leaving[None], score.reshape(1, users, items)


def solution(mesh):
    split = Mesh(mesh.devices.reshape(4, 16, 4, 2), ("segment",) + SHARD)
    in_specs = (
        P(SHARD, None),
        P(SHARD, None),
        P("segment", SHARD, None),
        P("segment", SHARD, None),
        P("segment", SHARD, None),
        P("segment", SHARD, None),
        P("segment", None),
        P("segment", SHARD, None),
        P("segment", SHARD),
    )
    out_specs = (P("segment", SHARD, None), P("segment", SHARD, None))
    return jax.shard_map(
        per_device, mesh=split, in_specs=in_specs, out_specs=out_specs, check_vma=False
    )
```

```python
import math

import jax
import jax.numpy as jnp
from jax import lax
from jax.experimental import pallas as pl
from jax.experimental.pallas import tpu as pltpu
from jax.sharding import Mesh
from jax.sharding import PartitionSpec as P

HEADS = 8
BU = 2
CAP = 8
F32 = jnp.float32
BF16 = jnp.bfloat16
SHARD = ("z", "y", "core")
FROM_Z = (4, 0, -4, 8, 3, -1, -5, 7, 5, 1, -3, 9, 6, 2, -2, -6)


def vmem():
    return pl.BlockSpec(memory_space=pltpu.VMEM)


def request_kernel(shard_rows, ids_ref, request_ref, slot_ref):
    users, items = ids_ref.shape
    shards, capacity = request_ref.shape
    ids = ids_ref[...]
    owners = ids // shard_rows
    offsets = ids - owners * shard_rows
    owner_row = lax.broadcasted_iota(jnp.int32, (shards, items), 0)
    before = (
        lax.broadcasted_iota(jnp.int32, (items, items), 0)
        < lax.broadcasted_iota(jnp.int32, (items, items), 1)
    ).astype(BF16)
    place_row = lax.broadcasted_iota(jnp.int32, (capacity, items), 0)
    base = jnp.zeros((shards, 1), F32)
    high = jnp.zeros((shards, capacity), F32)
    low = jnp.zeros((shards, capacity), F32)
    for user in range(users):
        mine = owner_row == owners[user : user + 1, :]
        onehot = mine.astype(F32)
        onehot_low = onehot.astype(BF16)
        earlier = jnp.dot(onehot_low, before, preferred_element_type=F32) + base
        place = jnp.sum(onehot * earlier, axis=0, keepdims=True).astype(jnp.int32)
        base = base + jnp.sum(onehot, axis=1, keepdims=True)
        at_place = place_row == place
        offset = offsets[user : user + 1, :]
        offset_high = jnp.where(at_place, offset // 64, 0).astype(F32).astype(BF16)
        offset_low = jnp.where(at_place, offset % 64, 0).astype(F32).astype(BF16)
        contract = (((1,), (1,)), ((), ()))
        high = high + lax.dot_general(
            onehot_low, offset_high, contract, preferred_element_type=F32
        )
        low = low + lax.dot_general(
            onehot_low, offset_low, contract, preferred_element_type=F32
        )
        slot_ref[user : user + 1, :] = owners[user : user + 1, :] * capacity + place
    request_ref[...] = (high * 64.0 + low).astype(jnp.int32)


def table_kernel(arrived_ref, table_ref, rows_ref):
    shards, capacity, width = rows_ref.shape
    shard_rows = table_ref.shape[0]
    block = 32
    count = block * capacity
    diagonal = lax.broadcasted_iota(
        jnp.int32, (block, capacity, capacity), 1
    ) == lax.broadcasted_iota(jnp.int32, (block, capacity, capacity), 2)
    row = lax.broadcasted_iota(jnp.int32, (count, shard_rows), 1)
    for start in range(0, shards, block):
        asked = arrived_ref[start : start + block, :]
        spread = jnp.broadcast_to(asked[:, None, :], (block, capacity, capacity))
        column = jnp.sum(jnp.where(diagonal, spread, 0).astype(F32), axis=2, keepdims=True)
        column = column.astype(jnp.int32).reshape(count, 1)
        onehot = (row == column).astype(F32).astype(BF16)
        found = jnp.dot(onehot, table_ref[...], preferred_element_type=F32)
        rows_ref[start : start + block] = found.astype(BF16).reshape(block, capacity, width)


def list_kernel(
    count_ref,
    returned_ref,
    slot_ref,
    state_ref,
    gain_ref,
    listed_ref,
    state_out_ref,
    gain_out_ref,
    length_ref,
):
    users, items = slot_ref.shape
    state_out_ref[...] = state_ref[...]
    gain_out_ref[...] = gain_ref[...]
    owner = lax.broadcasted_iota(jnp.int32, length_ref.shape, 1) // items
    lengths = jnp.zeros(length_ref.shape, jnp.int32)
    for user in range(users):
        lengths = jnp.where(owner == user, count_ref[0, user], lengths)
    length_ref[...] = lengths
    slots = slot_ref[...]
    slot_row = lax.broadcasted_iota(jnp.int32, (returned_ref.shape[0], items), 0)
    returned = returned_ref[...]
    for user in range(users):
        onehot = (slot_row == slots[user : user + 1, :]).astype(F32).astype(BF16)
        listed_ref[user * items : (user + 1) * items, :] = lax.dot_general(
            onehot, returned, (((0,), (0,)), ((), ())), preferred_element_type=F32
        ).astype(BF16)


def section_step(state, keys, values, ask, back, gain, lengths):
    users, width = state.shape
    count = keys.shape[0]
    items = count // users
    head_size = width // HEADS
    rows = users * HEADS
    query = jnp.dot(state, ask(), preferred_element_type=F32).astype(BF16)
    spread = jnp.broadcast_to(query.astype(F32)[:, None, :], (users, HEADS, width)).reshape(
        rows, width
    )
    in_head = (
        lax.broadcasted_iota(jnp.int32, (rows, width), 1) // head_size
        == lax.broadcasted_iota(jnp.int32, (rows, width), 0) % HEADS
    )
    spread = jnp.where(in_head, spread, 0.0).astype(BF16)
    logits = lax.dot_general(
        spread, keys[...], (((1,), (1,)), ((), ())), preferred_element_type=F32
    ) * (1.0 / math.sqrt(head_size))
    column = lax.broadcasted_iota(jnp.int32, (rows, count), 1)
    owner = lax.broadcasted_iota(jnp.int32, (rows, count), 0) // HEADS
    live = (column // items == owner) & (column % items < lengths)
    weights = jnp.where(live, jax.nn.silu(logits), 0.0)
    score = jnp.sum(weights, axis=0, keepdims=True) * (1.0 / HEADS)
    mixed = jnp.dot(weights.astype(BF16), values[...], preferred_element_type=F32)
    mixed = jnp.where(in_head, mixed, 0.0).reshape(users, HEADS, width)
    attended = jnp.sum(mixed, axis=1)
    scale = lax.rsqrt(jnp.mean(attended * attended, axis=1, keepdims=True) + 1e-05)
    normed = (attended * scale * gain).astype(BF16)
    update = jnp.dot(normed, back(), preferred_element_type=F32)
    return (state.astype(F32) + update).astype(BF16), score


def place(pieces, weight_ref, sems):
    zs, ys, cores, _, _ = weight_ref.shape
    z, y, core = (lax.axis_index(name) for name in SHARD)
    for number, (piece, first, from_y, swapped) in enumerate(pieces):
        to_y = lax.rem(y + from_y, ys)
        to_core = lax.rem(core + swapped, cores)
        for index in range(piece.shape[0]):
            to_z = lax.rem(z + FROM_Z[first + index] + zs, zs)
            pltpu.make_async_copy(
                piece.at[index], weight_ref.at[to_z, to_y, to_core], sems.at[number]
            ).start()


def wait_placed(pieces, weight_ref, sems):
    for number, (piece, *_) in enumerate(pieces):
        whole = weight_ref.at[pl.ds(0, piece.shape[0]), 0, 0]
        pltpu.make_async_copy(piece, whole, sems.at[number]).wait()


def place_kernel(*refs):
    *pieces, weight_ref, sems = refs
    ys = weight_ref.shape[1]
    parts = ((ys - 1, 0), (1, 0), (0, 1))
    kinds = [(piece, 0, *part) for piece, part in zip(pieces, parts)]
    place(kinds, weight_ref, sems)
    wait_placed(kinds, weight_ref, sems)


def item_kernel(
    column_ref,
    below_ref,
    above_ref,
    low_ref,
    high_ref,
    low_swapped_ref,
    high_swapped_ref,
    placed_ref,
    listed_ref,
    state_ref,
    gain_ref,
    length_ref,
    key_ref,
    value_ref,
    weight_ref,
    next_ref,
    score_ref,
    sems,
    load_sems,
):
    zs, ys, cores, _, _ = weight_ref.shape
    depth = width = key_ref.shape[1]
    emb = listed_ref.shape[1]
    half = zs // 2
    kinds = (
        (column_ref, 0, 0, 0),
        (below_ref, 0, ys - 1, 1),
        (above_ref, 0, 1, 1),
        (low_ref, 0, 2, 0),
        (high_ref, half, 2, 0),
        (low_swapped_ref, 0, 2, 1),
        (high_swapped_ref, half, 2, 1),
    )
    place(kinds, weight_ref, sems)
    y, core = lax.axis_index("y"), lax.axis_index("core")
    copies = []
    for part, (first, size) in enumerate(
        ((4 * width, emb), (0, 2 * width), (2 * width, 2 * width))
    ):
        mine = []
        for number, (from_y, from_core) in enumerate(
            ((ys - 1, 0), (1, 0), (0, 1))
        ):
            at = (
                slice(None),
                lax.rem(y + from_y, ys),
                lax.rem(core + from_core, cores),
                slice(None),
                pl.ds(first, size),
            )
            copy = pltpu.make_async_copy(
                placed_ref.at[at], weight_ref.at[at], load_sems.at[part, number]
            )
            copy.start()
            mine.append(copy)
        copies.append(mine)

    def weight(first, size):
        return weight_ref[:, :, :, :, first : first + size].reshape(depth, size)

    wait_placed(kinds, weight_ref, sems)
    for copy in copies[0]:
        copy.wait()
    listed = listed_ref[...]
    packed = weight(4 * width, emb)
    split = depth // emb
    lifted = []
    for part in range(split):
        pick = (
            lax.broadcasted_iota(jnp.int32, (emb, depth), 0) * split + part
            == lax.broadcasted_iota(jnp.int32, (emb, depth), 1)
        )
        lift = jnp.dot(
            pick.astype(F32).astype(BF16), packed, preferred_element_type=F32
        ).astype(BF16)
        lifted.append(
            jax.nn.silu(jnp.dot(listed, lift, preferred_element_type=F32)).astype(BF16)
        )
    lifted = jnp.concatenate(lifted, axis=1)
    for copy in copies[1]:
        copy.wait()
    block = 512
    for first in range(0, 2 * width, block):
        made = jnp.dot(lifted, weight(first, block), preferred_element_type=F32).astype(BF16)
        if first < width:
            key_ref[:, first : first + block] = made
        else:
            value_ref[:, first - width : first - width + block] = made
    for copy in copies[2]:
        copy.wait()
    next_ref[...], score_ref[...] = section_step(
        state_ref[...],
        key_ref,
        value_ref,
        lambda: weight(2 * width, width),
        lambda: weight(3 * width, width),
        gain_ref[...],
        length_ref[...],
    )


def section_kernel(
    state_ref, key_ref, value_ref, weight_ref, gain_ref, length_ref, *others
):
    next_ref, score_ref = others[-2:]
    earlier = (len(others) - 2) // 2
    width = state_ref.shape[2]
    state, score = section_step(
        state_ref[0],
        key_ref,
        value_ref,
        lambda: weight_ref[:, 2 * width : 3 * width],
        lambda: weight_ref[:, 3 * width : 4 * width],
        gain_ref[...],
        length_ref[...],
    )
    segment_index = lax.axis_index("segment") if earlier else None
    for step in range(earlier):
        mine = segment_index == step
        state = jnp.where(mine, others[step][...], state)
        score = jnp.where(mine, others[earlier + step][...], score)
    next_ref[...] = state
    score_ref[...] = score


def per_device(
    item_table, user_states, w_lift, w_pair, w_ask, w_back, norm_gains, item_ids, lengths
):
    segment_count = lax.axis_size("segment")
    zs, ys, cores = (lax.axis_size(name) for name in SHARD)
    shards = zs * ys * cores
    users, width = user_states.shape
    items = item_ids.shape[2]
    shard_rows, emb = item_table.shape
    depth = w_ask.shape[1]
    small, big, wide = (pltpu.CompilerParams(vmem_limit_bytes=size << 20) for size in (12, 34, 44))

    own = jnp.concatenate(
        [w_pair[0], w_ask[0], w_back[0], w_lift[0].reshape(depth, emb)], axis=1
    )
    def moved(block, axis, distance):
        size = lax.axis_size(axis)
        return lax.ppermute(block, axis, [(i, (i + distance) % size) for i in range(size)])

    request, slots = pl.pallas_call(
        lambda *refs: request_kernel(shard_rows, *refs),
        out_shape=(
            jax.ShapeDtypeStruct((shards, CAP), jnp.int32),
            jax.ShapeDtypeStruct((users, items), jnp.int32),
        ),
        in_specs=[vmem()],
        out_specs=(vmem(), vmem()),
        compiler_params=small,
        name="request",
    )(item_ids[0])
    arrived = lax.all_to_all(
        request.reshape(shards, 1, CAP), SHARD, split_axis=0, concat_axis=0, tiled=True
    )
    own = own[None]
    far = jnp.concatenate([moved(own, "z", -4), own, moved(own, "z", 4), moved(own, "z", 8)])
    near = (
        moved(far, "z", 1),
        moved(far, "z", -1),
        moved(far[:2], "z", -2),
        moved(far[1:3], "z", 2),
    )
    near, arrived = lax.optimization_barrier((near, arrived))
    column = jnp.concatenate([far, *near])
    half = zs // 2
    below, above = moved(column, "y", 1), moved(column, "y", -1)
    across = (moved(below[:half], "y", 1), moved(above[half:], "y", -1))
    early = [below, above]
    early = early + [moved(column, "core", 1)]
    swapped = (moved(below, "core", 1), moved(above, "core", 1))
    found = pl.pallas_call(
        table_kernel,
        out_shape=jax.ShapeDtypeStruct((shards, CAP, emb), BF16),
        in_specs=[vmem(), vmem()],
        out_specs=vmem(),
        compiler_params=small,
        name="table",
    )(arrived.reshape(shards, CAP), item_table)
    returned = lax.all_to_all(found, SHARD, split_axis=0, concat_axis=0, tiled=True)

    weights = pl.pallas_call(
        place_kernel,
        out_shape=jax.ShapeDtypeStruct((zs, ys, cores, depth, own.shape[2]), BF16),
        in_specs=[pl.BlockSpec(memory_space=pl.ANY)] * len(early),
        out_specs=pl.BlockSpec(memory_space=pltpu.HBM),
        scratch_shapes=[pltpu.SemaphoreType.DMA((len(early),))],
        compiler_params=wide,
        cost_estimate=pl.CostEstimate(flops=0, bytes_accessed=14_000_000, transcendentals=0),
        name="place",
    )(*early)
    across, weights = lax.optimization_barrier((across, weights))
    late = [column, *swapped, *across, *(moved(piece, "core", 1) for piece in across)]

    smem = pl.BlockSpec(memory_space=pltpu.SMEM)
    listed, entering, gains, length_row = pl.pallas_call(
        list_kernel,
        out_shape=(
            jax.ShapeDtypeStruct((users * items, emb), BF16),
            jax.ShapeDtypeStruct(user_states.shape, BF16),
            jax.ShapeDtypeStruct(norm_gains.shape, F32),
            jax.ShapeDtypeStruct((1, users * items), jnp.int32),
        ),
        in_specs=[smem] + [vmem()] * 4,
        out_specs=(vmem(),) * 4,
        compiler_params=small,
        name="list",
    )(lengths, returned.reshape(shards * CAP, emb), slots, user_states, norm_gains)

    section_shape = (
        jax.ShapeDtypeStruct((users, width), BF16),
        jax.ShapeDtypeStruct((1, users * items), F32),
    )
    keys, values, weights, leaving, score = pl.pallas_call(
        item_kernel,
        out_shape=(
            jax.ShapeDtypeStruct((users * items, width), BF16),
            jax.ShapeDtypeStruct((users * items, width), BF16),
            jax.ShapeDtypeStruct((zs, ys, cores, depth, own.shape[2]), BF16),
        )
        + section_shape,
        in_specs=[pl.BlockSpec(memory_space=pl.ANY)] * len(late)
        + [pl.BlockSpec(memory_space=pltpu.HBM)]
        + [vmem()] * 4,
        out_specs=(vmem(),) * 5,
        scratch_shapes=[
            pltpu.SemaphoreType.DMA((len(late),)),
            pltpu.SemaphoreType.DMA((3, 3)),
        ],
        compiler_params=big,
        name="item",
    )(*late, weights, listed, entering, gains, length_row)
    weights = weights.reshape(shards * depth, own.shape[2])

    even, odd = [[0, 1], [2, 3]], [[1, 2], [0, 3]]
    states, scores = [leaving], [score]
    for step in range(1, segment_count):
        entering = lax.all_gather(
            leaving, "segment", axis=0, axis_index_groups=(even, odd)[step % 2 == 0]
        )
        earlier = (*states, *scores) if step + 1 == segment_count else ()
        leaving, score = pl.pallas_call(
            section_kernel,
            out_shape=section_shape,
            in_specs=[vmem()] * (6 + len(earlier)),
            out_specs=(vmem(), vmem()),
            compiler_params=small,
            name="section",
        )(
            entering,
            keys,
            values,
            weights,
            gains,
            length_row,
            *earlier,
        )
        states.append(leaving)
        scores.append(score)
    return leaving[None], score.reshape(1, users, items)


def solution(mesh):
    split = Mesh(mesh.devices.reshape(4, 16, 4, 2), ("segment",) + SHARD)
    in_specs = (
        P(SHARD, None),
        P(SHARD, None),
        P("segment", SHARD, None),
        P("segment", SHARD, None),
        P("segment", SHARD, None),
        P("segment", SHARD, None),
        P("segment", None),
        P("segment", SHARD, None),
        P("segment", SHARD),
    )
    out_specs = (P("segment", SHARD, None), P("segment", SHARD, None))
    return jax.shard_map(
        per_device, mesh=split, in_specs=in_specs, out_specs=out_specs, check_vma=False
    )
```
